256 devices in a mesh: rows: 8 (over y, core), chan: 32 (over x, z).
Axes of the slice: x: 4, y: 4, z: 8, core: 2. Of those that a mesh axis runs over, the one named last changes fastest.
Arguments:
- features: bfloat16 [512, 1536, 256], P('rows', 'chan'), may hold values from -6 to 6
- mixing: float32 [3, 512, 256], P(None, 'rows'), may hold values from 0 to 1, as said below
- decay_rate: float32 [512, 256], P('rows'), may hold values from 0 to 0.5, as said below
- gate_input: bfloat16 [512, 1536, 256], P('rows', 'chan'), may hold values from -6 to 6
- out_weight: bfloat16 [1536, 1536], replicated, may hold values from -0.15625 to 0.15625
Outputs:
- projected: bfloat16 [512, 1536, 256], P(('rows', 'chan'))
The draws below stay inside these ranges and needn't reach their ends.
Inputs may be any that keep to these rules, and one draw needn't show every extreme that they name: `mixing`: at every row and column the three weights are positive where their neighbour exists, the left weight is zero at column 0 and the right weight at column 255, and the three sum to one. `decay_rate`: every entry is positive.
All inputs are finite; a program needn't handle non-finite values.
Results may differ from the reference program's by a relative error of at most 0.0049.
Values may be sent and summed in bfloat16 or wider, within the bound.
No kernel may reach another device: no remote copies, remote signals or barrier semaphores. Data moves between devices by JAX's collectives and lax.ppermute only.
A program may use at most 128 MiB of HBM per device.

```python
import jax
import jax.numpy as jnp
from jax import lax

C = 1536
STRIP_COLUMNS = 256
STRIP_ROWS = 512


def draw_mixing(key, part):
    random_keys = jax.random.split(jax.random.fold_in(key, 11), 3)
    side_low = 0.2
    side_high = 1.0
    left_w = jax.random.uniform(random_keys[0], (STRIP_ROWS, STRIP_COLUMNS), jnp.float32, side_low, side_high)
    right_w = jax.random.uniform(random_keys[1], (STRIP_ROWS, STRIP_COLUMNS), jnp.float32, side_low, side_high)
    mid_w = jax.random.uniform(random_keys[2], (STRIP_ROWS, STRIP_COLUMNS), jnp.float32, 1.0, 2.0)
    column = jnp.arange(STRIP_COLUMNS)[None, :]
    left_w = jnp.where(column == 0, 0.0, left_w)
    right_w = jnp.where(column == STRIP_COLUMNS - 1, 0.0, right_w)
    totals = left_w + mid_w + right_w
    return jnp.stack([left_w / totals, mid_w / totals, right_w / totals])


def draw_decay_rate(key, part):
    random_keys = jax.random.split(jax.random.fold_in(key, 23), 7)
    share = 0.5
    picked = jax.random.uniform(random_keys[0], (STRIP_COLUMNS,)) < share
    fast_rate = jax.random.uniform(random_keys[1], (STRIP_COLUMNS,), jnp.float32, 0.02, 0.04)
    slow_rate = jax.random.uniform(random_keys[2], (STRIP_COLUMNS,), jnp.float32, 0.05, 0.5) / STRIP_ROWS
    base_rate = jnp.where(picked, fast_rate, slow_rate)
    row_factor = jnp.exp(jax.random.uniform(random_keys[3], (STRIP_ROWS, 1), jnp.float32, -0.7, 0.7))
    cell_factor = jax.random.uniform(random_keys[4], (STRIP_ROWS, STRIP_COLUMNS), jnp.float32, 0.6, 1.4)
    decay_rates = base_rate[None, :] * row_factor * cell_factor
    spike_row_list = jax.random.randint(random_keys[5], (3,), 0, STRIP_ROWS)
    spike_event = jnp.zeros((STRIP_ROWS,), jnp.float32).at[spike_row_list].set(1.0)
    spike_frequency = jax.random.uniform(random_keys[6], (STRIP_ROWS, STRIP_COLUMNS), jnp.float32, 0.2, 0.5)
    decay_rates = jnp.where(spike_event[:, None] > 0.5, spike_frequency, decay_rates)
    return jnp.minimum(decay_rates, 0.5)


def level_of(stream_key, shape, cuts, smallest, top_value):
    gain, own = 1.0, jax.random.fold_in(stream_key, 6)
    for dim, shards_of in cuts:
        draws = jnp.exp(jax.random.uniform(jax.random.fold_in(own, dim), (shards_of,), jnp.float32, smallest / len(cuts), top_value / len(cuts)))
        gain = gain * jnp.repeat(draws, shape[dim] // shards_of).reshape([-1 if axis == dim else 1 for axis in range(len(shape))])
    return gain


def normal_values(key, dims, deviation, most, shards=(), held_as=jnp.bfloat16):
    values = jax.random.normal(key, dims, jnp.float32) * deviation
    if len(shards) > 0:
        values = level_of(key, dims, shards, -0.22, 0.18) * values
    return jnp.clip(values, min=-most, max=most).astype(held_as)


def setup_inputs(seed: int = 0) -> dict:
    key_list = jax.random.split(jax.random.key(seed), 6)
    return {
        "features": normal_values(key_list[0], (STRIP_ROWS, C, STRIP_COLUMNS), 1.0, 6.0, ((0, 8), (1, 32))),
        "mixing": draw_mixing(jax.random.fold_in(key_list[5], 71), 0),
        "decay_rate": draw_decay_rate(jax.random.fold_in(key_list[5], 71), 0),
        "gate_input": normal_values(key_list[3], (STRIP_ROWS, C, STRIP_COLUMNS), 1.0, 6.0, ((0, 8), (1, 32))),
        "out_weight": normal_values(key_list[4], (C, C), C ** -0.5, 0.15625),
    }


def reference(features, mixing, decay_rate, gate_input, out_weight):
    retain = 1.0 - decay_rate
    left_all = retain * mixing[0]
    mid_all = retain * mixing[1]
    right_all = retain * mixing[2]
    scale_all = jnp.sqrt(decay_rate)

    def advance(hidden_st, row_in):
        feat_row, gate_row, left_row, mid_row, right_row, scale_row = row_in
        edge_col = jnp.zeros((hidden_st.shape[0], 1), jnp.float32)
        before_col = jnp.concatenate([edge_col, hidden_st[:, :-1]], axis=1)
        after_col = jnp.concatenate([hidden_st[:, 1:], edge_col], axis=1)
        hidden_st = left_row[None] * before_col + mid_row[None] * hidden_st + right_row[None] * after_col
        hidden_st = hidden_st + scale_row[None] * feat_row.astype(jnp.float32)
        gated = (hidden_st * jax.nn.silu(gate_row.astype(jnp.float32))).astype(jnp.bfloat16)
        out_row = jnp.dot(out_weight, gated, preferred_element_type=jnp.float32).astype(jnp.bfloat16)
        return (hidden_st, out_row)
    start_st = jnp.zeros((features.shape[1], features.shape[2]), jnp.float32)
    _, projected = lax.scan(advance, start_st, (features, gate_input, left_all, mid_all, right_all, scale_all))
    return projected
```

```python
import jax
import jax.numpy as jnp
from jax import lax
from jax.experimental import pallas as pl
from jax.experimental.pallas import tpu as pltpu
from jax.sharding import PartitionSpec as P

CHUNK = 16
ROW_BLOCK = 8


def stencil(state, left_w, mid_w, right_w):
    width = state.shape[1]
    before_col = pltpu.roll(state, 1, 1)
    after_col = pltpu.roll(state, width - 1, 1)
    return left_w * before_col + mid_w * state + right_w * after_col


def operator_kernel(mix_ref, decay_ref, op_ref, left_ref, mid_ref, right_ref, in_ref):
    decay = decay_ref[...]
    retain = 1.0 - decay
    left_ref[...] = retain * mix_ref[0]
    mid_ref[...] = retain * mix_ref[1]
    right_ref[...] = retain * mix_ref[2]
    in_ref[...] = jnp.sqrt(decay)
    rows, width = decay.shape
    group = 64
    for part in range(width // group):
        source = lax.broadcasted_iota(jnp.int32, (group, width), 0) + part * group
        column = lax.broadcasted_iota(jnp.int32, (group, width), 1)
        start = jnp.where(source == column, 1.0, 0.0).astype(jnp.float32)

        def step(i, state):
            row = pl.ds(i, 1)
            return stencil(state, left_ref[row, :], mid_ref[row, :], right_ref[row, :])

        final = lax.fori_loop(0, rows, step, start, unroll=4)
        op_ref[part * group : (part + 1) * group, :] = final.astype(op_ref.dtype)


def operator_of(mixing, decay_rate):
    _, rows, width = mixing.shape
    coef = jax.ShapeDtypeStruct((rows, width), jnp.float32)
    return pl.pallas_call(
        operator_kernel,
        out_shape=(jax.ShapeDtypeStruct((width, width), jnp.bfloat16), coef, coef, coef, coef),
        cost_estimate=pl.CostEstimate(
            flops=5 * rows * width * width, bytes_accessed=8 * rows * width * 4, transcendentals=0
        ),
        name="operator",
    )(mixing, decay_rate)


def ending_kernel(feat_ref, left_ref, mid_ref, right_ref, in_ref, end_ref):
    @pl.when(pl.program_id(0) == 0)
    def _():
        end_ref[...] = jnp.zeros_like(end_ref)

    state = end_ref[...]
    for j in range(feat_ref.shape[0]):
        row = pl.ds(j, 1)
        push = in_ref[row, :] * feat_ref[j].astype(jnp.float32)
        state = stencil(state, left_ref[row, :], mid_ref[row, :], right_ref[row, :]) + push
    end_ref[...] = state


def ending(features, coefs):
    rows, channels, width = features.shape
    coef_spec = pl.BlockSpec((ROW_BLOCK, width), lambda i: (i, 0))
    return pl.pallas_call(
        ending_kernel,
        grid=(rows // ROW_BLOCK,),
        in_specs=[pl.BlockSpec((ROW_BLOCK, channels, width), lambda i: (i, 0, 0))] + [coef_spec] * 4,
        out_specs=pl.BlockSpec((channels, width), lambda i: (0, 0)),
        out_shape=jax.ShapeDtypeStruct((channels, width), jnp.float32),
        cost_estimate=pl.CostEstimate(
            flops=7 * rows * channels * width, bytes_accessed=2 * rows * channels * width, transcendentals=0
        ),
        name="ending",
    )(features, *coefs)


def gated_kernel(feat_ref, gate_ref, start_ref, left_ref, mid_ref, right_ref, in_ref, out_ref, state_ref):
    @pl.when(pl.program_id(0) == 0)
    def _():
        state_ref[...] = start_ref[...]

    state = state_ref[...]
    for j in range(feat_ref.shape[0]):
        row = pl.ds(j, 1)
        push = in_ref[row, :] * feat_ref[j].astype(jnp.float32)
        state = stencil(state, left_ref[row, :], mid_ref[row, :], right_ref[row, :]) + push
        gate = gate_ref[j].astype(jnp.float32)
        out_ref[j] = (state * (gate / (1.0 + jnp.exp(-gate)))).astype(out_ref.dtype)
    state_ref[...] = state


def gated(features, gate_input, incoming, coefs, part):
    rows, channels, width = features.shape
    coef_spec = pl.BlockSpec((ROW_BLOCK, width), lambda i: (i, 0))
    wide_spec = pl.BlockSpec((ROW_BLOCK, CHUNK, width), lambda i: (i, part, 0))
    return pl.pallas_call(
        gated_kernel,
        grid=(rows // ROW_BLOCK,),
        in_specs=[wide_spec, wide_spec, pl.BlockSpec((CHUNK, width), lambda i: (part, 0))] + [coef_spec] * 4,
        out_specs=pl.BlockSpec((ROW_BLOCK, CHUNK, width), lambda i: (i, 0, 0)),
        out_shape=jax.ShapeDtypeStruct((rows, CHUNK, width), jnp.bfloat16),
        scratch_shapes=[pltpu.VMEM((CHUNK, width), jnp.float32)],
        cost_estimate=pl.CostEstimate(
            flops=12 * rows * CHUNK * width, bytes_accessed=6 * rows * CHUNK * width, transcendentals=rows * CHUNK * width
        ),
        name="gated",
    )(features, gate_input, incoming, *coefs)


def passed_on(value, shift, first, count):
    return lax.ppermute(value, "rows", [(i, i + shift) for i in range(first, count - shift)])


def shards(count, features, mixing, decay_rate, gate_input, out_weight):
    rows, channels, width = features.shape
    operator, *coefs = operator_of(mixing, decay_rate)
    ops = {shift: passed_on(operator, shift, 1, count) for shift in range(1, count - 1)}
    end = ending(features, coefs)
    ends = {shift: passed_on(end, shift, 0, count) for shift in range(1, count)}

    incoming = ends[count - 1]
    for shift in range(count - 2, 0, -1):
        high = incoming.astype(jnp.bfloat16)
        low = (incoming - high.astype(jnp.float32)).astype(jnp.bfloat16)
        both = jnp.dot(jnp.concatenate([high, low]), ops[shift], preferred_element_type=jnp.float32)
        incoming = both[:channels] + both[channels:] + ends[shift]

    parts = channels // CHUNK
    group = out_weight.reshape(out_weight.shape[0], -1, parts, CHUNK)
    total = 0.0
    for part in range(parts):
        mixed = gated(features, gate_input, incoming, coefs, part)
        here = lax.all_to_all(mixed, "chan", split_axis=0, concat_axis=1, tiled=True)
        weight = group[:, :, part, :].reshape(out_weight.shape[0], -1)
        total = total + jnp.einsum("oc,rcw->row", weight, here, preferred_element_type=jnp.float32)
    return total.astype(jnp.bfloat16)


def solution(mesh):
    in_specs = (
        P("rows", "chan", None),
        P(None, "rows", None),
        P("rows", None),
        P("rows", "chan", None),
        P(),
    )
    out_specs = P(("rows", "chan"), None, None)

    def whole(features, mixing, decay_rate, gate_input, out_weight):
        return shards(mesh.shape["rows"], features, mixing, decay_rate, gate_input, out_weight)

    return jax.shard_map(whole, mesh=mesh, in_specs=in_specs, out_specs=out_specs, check_vma=False)
```

```python
import jax
import jax.numpy as jnp
from jax import lax
from jax.experimental import pallas as pl
from jax.experimental.pallas import tpu as pltpu
from jax.sharding import PartitionSpec as P

STEP_ROWS = 8
HALF = 128
REACH = 32
HIGHEST = lax.Precision.HIGHEST


def stencil(state, left_w, mid_w, right_w):
    width = state.shape[1]
    before_col = pltpu.roll(state, 1, 1)
    after_col = pltpu.roll(state, width - 1, 1)
    return left_w * before_col + mid_w * state + right_w * after_col


def diagonal(first, count, left, width):
    source = lax.broadcasted_iota(jnp.int32, (count, width), 0) + first
    column = lax.broadcasted_iota(jnp.int32, (count, width), 1) + left
    return jnp.where(source == column, 1.0, 0.0).astype(jnp.float32)


def operator_kernel(
    mix_ref, decay_ref, op_ref, early_ref, late_ref, left_ref, mid_ref, right_ref, in_ref, left_cut_ref, right_cut_ref
):
    rows, width = decay_ref.shape
    decay = decay_ref[...]
    retain = 1.0 - decay
    column = lax.broadcasted_iota(jnp.int32, (rows, width), 1)
    left_w = retain * mix_ref[0]
    right_w = retain * mix_ref[2]
    left_ref[...] = left_w
    mid_ref[...] = retain * mix_ref[1]
    right_ref[...] = right_w
    in_ref[...] = jnp.sqrt(decay)
    left_cut_ref[...] = jnp.where(column == HALF, 0.0, left_w)
    right_cut_ref[...] = jnp.where(column == HALF - 1, 0.0, right_w)

    inner = HALF - REACH
    outs = (early_ref, late_ref)
    for out in outs:
        out[0:inner, HALF:width] = jnp.zeros((inner, width - HALF), jnp.float32)
        out[width - inner : width, 0:HALF] = jnp.zeros((inner, HALF), jnp.float32)

    def sweep(first, count, left, right, lefts, rights):
        lanes = slice(left, right)

        def step(i, states):
            news = []
            for half in range(2):
                row = pl.ds(i + half * REACH, 1)
                weights = [ref[row, :][:, lanes] for ref in (lefts, mid_ref, rights)]
                news.append(stencil(states[half], *weights))
            return tuple(news)

        start = diagonal(first, count, left, right - left)
        finals = lax.fori_loop(0, REACH, step, (start, start), unroll=4)
        for out, final in zip(outs, finals):
            out[first : first + count, lanes] = final

    sweep(0, inner, 0, HALF, left_ref, right_cut_ref)
    sweep(width - inner, inner, HALF, width, left_cut_ref, right_ref)
    sweep(inner, 2 * REACH, 0, width, left_ref, right_ref)
    op_ref[...] = jnp.dot(
        early_ref[...], late_ref[...], precision=HIGHEST, preferred_element_type=jnp.float32
    ).astype(op_ref.dtype)


def operator_of(mixing, decay_rate):
    _, rows, width = mixing.shape
    square = jax.ShapeDtypeStruct((width, width), jnp.float32)
    coef = jax.ShapeDtypeStruct((rows, width), jnp.float32)
    return pl.pallas_call(
        operator_kernel,
        out_shape=(jax.ShapeDtypeStruct((width, width), jnp.bfloat16), square, square, coef, coef, coef, coef),
        scratch_shapes=[pltpu.VMEM((rows, width), jnp.float32)] * 2,
        cost_estimate=pl.CostEstimate(
            flops=5 * rows * width * width, bytes_accessed=8 * rows * width * 4, transcendentals=0
        ),
        name="operator",
    )(mixing, decay_rate)


def ending_kernel(feat_ref, left_ref, mid_ref, right_ref, in_ref, late_ref, early_end_ref, end_ref, state_ref):
    @pl.when(pl.program_id(0) == 0)
    def _():
        state_ref[...] = jnp.zeros_like(state_ref)

    states = [state_ref[0], state_ref[1]]
    for j in range(feat_ref.shape[1]):
        row = pl.ds(j, 1)
        for half in range(2):
            push = in_ref[half, row, :] * feat_ref[half, j].astype(jnp.float32)
            states[half] = (
                stencil(states[half], left_ref[half, row, :], mid_ref[half, row, :], right_ref[half, row, :]) + push
            )
    state_ref[0] = states[0]
    state_ref[1] = states[1]

    @pl.when(pl.program_id(0) == pl.num_programs(0) - 1)
    def _():
        early_end_ref[...] = states[0]
        end_ref[...] = states[1] + jnp.dot(
            states[0], late_ref[...], precision=HIGHEST, preferred_element_type=jnp.float32
        )


def ending(features, coefs, late):
    _, rows, channels, width = features.shape
    coef_spec = pl.BlockSpec((2, STEP_ROWS, width), lambda i: (0, i, 0))
    state = jax.ShapeDtypeStruct((channels, width), jnp.float32)
    state_spec = pl.BlockSpec((channels, width), lambda i: (0, 0))
    return pl.pallas_call(
        ending_kernel,
        grid=(rows // STEP_ROWS,),
        in_specs=[pl.BlockSpec((2, STEP_ROWS, channels, width), lambda i: (0, i, 0, 0))]
        + [coef_spec] * 4
        + [pl.BlockSpec((width, width), lambda i: (0, 0))],
        out_specs=(state_spec, state_spec),
        out_shape=(state, state),
        scratch_shapes=[pltpu.VMEM((2, channels, width), jnp.float32)],
        cost_estimate=pl.CostEstimate(
            flops=14 * rows * channels * width, bytes_accessed=4 * rows * channels * width, transcendentals=0
        ),
        name="ending",
    )(features, *coefs, late)


def gated_kernel(
    core_ref, my_ops_ref, their_ops_ref, my_ends_ref, their_ends_ref, early_ref, early_end_ref,
    feat_ref, gate_ref, left_ref, mid_ref, right_ref, in_ref, out_ref, state_ref,
):
    @pl.when(pl.program_id(0) == 0)
    def _():
        first = core_ref[0] == 0

        def applied(state, operator):
            high = state.astype(jnp.bfloat16)
            low = (state - high.astype(jnp.float32)).astype(jnp.bfloat16)
            out = jnp.dot(high, operator, preferred_element_type=jnp.float32)
            return out + jnp.dot(low, operator, preferred_element_type=jnp.float32)

        def pick(slot, core, mine, theirs):
            return jnp.where(first == (core == 0), mine[slot], theirs[slot])

        slots = my_ends_ref.shape[0]
        incoming = pick(slots - 1, 0, my_ends_ref, their_ends_ref)
        for slot, core in [(slots - 1, 1)] + [(s, c) for s in range(slots - 2, 0, -1) for c in range(2)]:
            incoming = applied(incoming, pick(slot, core, my_ops_ref, their_ops_ref))
            incoming = incoming + pick(slot, core, my_ends_ref, their_ends_ref)
        later = applied(incoming, their_ops_ref[0]) + their_ends_ref[0]
        incoming = jnp.where(first, incoming, later)
        state_ref[0] = incoming
        state_ref[1] = early_end_ref[...] + jnp.dot(
            incoming, early_ref[...], precision=HIGHEST, preferred_element_type=jnp.float32
        )

    states = [state_ref[0], state_ref[1]]
    for j in range(feat_ref.shape[1]):
        row = pl.ds(j, 1)
        for half in range(2):
            push = in_ref[half, row, :] * feat_ref[half, j].astype(jnp.float32)
            states[half] = (
                stencil(states[half], left_ref[half, row, :], mid_ref[half, row, :], right_ref[half, row, :]) + push
            )
            gate = gate_ref[half, j].astype(jnp.float32)
            out_ref[half, j] = (states[half] * (gate / (1.0 + jnp.exp(-gate)))).astype(out_ref.dtype)
    state_ref[0] = states[0]
    state_ref[1] = states[1]


def gated(core, my_ops, their_ops, my_ends, their_ends, early, early_end, features, gate_input, coefs):
    _, rows, channels, width = features.shape

    def fixed(array):
        return pl.BlockSpec(array.shape, lambda i, *_: (0,) * array.ndim)

    coef_spec = pl.BlockSpec((2, STEP_ROWS, width), lambda i, *_: (0, i, 0))
    wide_spec = pl.BlockSpec((2, STEP_ROWS, channels, width), lambda i, *_: (0, i, 0, 0))
    starts = (my_ops, their_ops, my_ends, their_ends, early, early_end)
    return pl.pallas_call(
        gated_kernel,
        grid_spec=pltpu.PrefetchScalarGridSpec(
            num_scalar_prefetch=1,
            grid=(rows // STEP_ROWS,),
            in_specs=[fixed(a) for a in starts] + [wide_spec, wide_spec] + [coef_spec] * 4,
            out_specs=wide_spec,
            scratch_shapes=[pltpu.VMEM((2, channels, width), jnp.float32)],
        ),
        out_shape=jax.ShapeDtypeStruct(features.shape, jnp.bfloat16),
        cost_estimate=pl.CostEstimate(
            flops=24 * rows * channels * width,
            bytes_accessed=12 * rows * channels * width,
            transcendentals=4 * rows * channels * width,
        ),
        name="gated",
    )(core, *starts, features, gate_input, *coefs)


def project_kernel(weight_ref, gated_ref, out_ref):
    here = gated_ref[...]
    here = here.reshape(here.shape[0] * here.shape[2], here.shape[3])
    out_ref[0] = jnp.dot(weight_ref[...], here, preferred_element_type=jnp.float32).astype(out_ref.dtype)


def project(out_weight, gathered):
    peers, rows, channels, width = gathered.shape
    outs = out_weight.shape[0]
    tile = outs // 3
    return pl.pallas_call(
        project_kernel,
        grid=(outs // tile, rows),
        in_specs=[
            pl.BlockSpec((tile, out_weight.shape[1]), lambda o, r: (o, 0)),
            pl.BlockSpec((peers, 1, channels, width), lambda o, r: (0, r, 0, 0)),
        ],
        out_specs=pl.BlockSpec((1, tile, width), lambda o, r: (r, o, 0)),
        out_shape=jax.ShapeDtypeStruct((rows, outs, width), jnp.bfloat16),
        cost_estimate=pl.CostEstimate(
            flops=2 * rows * outs * outs * width, bytes_accessed=4 * outs * outs, transcendentals=0
        ),
        name="project",
    )(out_weight, gathered)


def shards(slabs, peers, features, mixing, decay_rate, gate_input, out_weight):
    rows, channels, width = features.shape
    chips = slabs // 2
    features = features.reshape(2, rows // 2, channels, width)
    gate_input = gate_input.reshape(2, rows // 2, channels, width)
    core = (lax.axis_index("rows") % 2).astype(jnp.int32).reshape(1)

    def back(value, shift, first):
        return lax.ppermute(value, "rows", [(i, i + 2 * shift) for i in range(first, slabs - 2 * shift)])

    def swapped(value):
        return lax.ppermute(value, "rows", [(i, i ^ 1) for i in range(slabs)])

    operator, early, late, *coefs = operator_of(mixing, decay_rate)
    coefs = [c.reshape(2, rows // 2, width) for c in coefs]
    my_ops = jnp.stack([operator] + [back(operator, shift, 1) for shift in range(1, chips)])
    early_end, end = ending(features, coefs, late)
    my_ends = jnp.stack([end] + [back(end, shift, 0) for shift in range(1, chips)])
    their_ops = swapped(my_ops)
    their_ends = swapped(my_ends)

    mixed = gated(core, my_ops, their_ops, my_ends, their_ends, early, early_end, features, gate_input, coefs)
    mixed = mixed.reshape(peers, rows // peers, channels, width)
    return project(out_weight, lax.all_to_all(mixed, "chan", split_axis=0, concat_axis=0, tiled=True))


def solution(mesh):
    in_specs = (
        P("rows", "chan", None),
        P(None, "rows", None),
        P("rows", None),
        P("rows", "chan", None),
        P(),
    )
    out_specs = P(("rows", "chan"), None, None)

    def whole(features, mixing, decay_rate, gate_input, out_weight):
        return shards(
            mesh.shape["rows"], mesh.shape["chan"], features, mixing, decay_rate, gate_input, out_weight
        )

    return jax.shard_map(whole, mesh=mesh, in_specs=in_specs, out_specs=out_specs, check_vma=False)
```

```python
import jax
import jax.numpy as jnp
from jax import lax
from jax.experimental import pallas as pl
from jax.experimental.pallas import tpu as pltpu
from jax.sharding import PartitionSpec as P

STEP_ROWS = 8
HALF = 128
REACH = 32
TILES = 4
VMEM_LIMIT = 16 * 1024 * 1024
HIGHEST = lax.Precision.HIGHEST


def stencil(state, left_w, mid_w, right_w):
    width = state.shape[1]
    before_col = pltpu.roll(state, 1, 1)
    after_col = pltpu.roll(state, width - 1, 1)
    return left_w * before_col + mid_w * state + right_w * after_col


def diagonal(first, count, left, width):
    source = lax.broadcasted_iota(jnp.int32, (count, width), 0) + first
    column = lax.broadcasted_iota(jnp.int32, (count, width), 1) + left
    return jnp.where(source == column, 1.0, 0.0).astype(jnp.float32)


def operator_kernel(
    mix_ref, decay_ref, op_ref, early_ref, late_ref, left_ref, mid_ref, right_ref, in_ref, left_cut_ref, right_cut_ref
):
    rows, width = decay_ref.shape
    decay = decay_ref[...]
    retain = 1.0 - decay
    column = lax.broadcasted_iota(jnp.int32, (rows, width), 1)
    left_w = retain * mix_ref[0]
    right_w = retain * mix_ref[2]
    left_ref[...] = left_w
    mid_ref[...] = retain * mix_ref[1]
    right_ref[...] = right_w
    in_ref[...] = jnp.sqrt(decay)
    left_cut_ref[...] = jnp.where(column == HALF, 0.0, left_w)
    right_cut_ref[...] = jnp.where(column == HALF - 1, 0.0, right_w)

    inner = HALF - REACH
    outs = (early_ref, late_ref)
    for out in outs:
        out[0:inner, HALF:width] = jnp.zeros((inner, width - HALF), jnp.float32)
        out[width - inner : width, 0:HALF] = jnp.zeros((inner, HALF), jnp.float32)

    def sweep(first, count, left, right, lefts, rights):
        lanes = slice(left, right)

        def step(i, states):
            news = []
            for half in range(2):
                row = pl.ds(i + half * REACH, 1)
                weights = [ref[row, :][:, lanes] for ref in (lefts, mid_ref, rights)]
                news.append(stencil(states[half], *weights))
            return tuple(news)

        start = diagonal(first, count, left, right - left)
        finals = lax.fori_loop(0, REACH, step, (start, start), unroll=4)
        for out, final in zip(outs, finals):
            out[first : first + count, lanes] = final

    sweep(0, inner, 0, HALF, left_ref, right_cut_ref)
    sweep(width - inner, inner, HALF, width, left_cut_ref, right_ref)
    sweep(inner, 2 * REACH, 0, width, left_ref, right_ref)
    op_ref[...] = jnp.dot(
        early_ref[...], late_ref[...], precision=HIGHEST, preferred_element_type=jnp.float32
    ).astype(op_ref.dtype)


def operator_of(mixing, decay_rate):
    _, rows, width = mixing.shape
    square = jax.ShapeDtypeStruct((width, width), jnp.float32)
    coef = jax.ShapeDtypeStruct((rows, width), jnp.float32)
    return pl.pallas_call(
        operator_kernel,
        out_shape=(jax.ShapeDtypeStruct((width, width), jnp.bfloat16), square, square, coef, coef, coef, coef),
        scratch_shapes=[pltpu.VMEM((rows, width), jnp.float32)] * 2,
        cost_estimate=pl.CostEstimate(
            flops=5 * rows * width * width, bytes_accessed=8 * rows * width * 4, transcendentals=0
        ),
        compiler_params=pltpu.CompilerParams(vmem_limit_bytes=VMEM_LIMIT),
        name="operator",
    )(mixing, decay_rate)


def ending_kernel(feat_ref, left_ref, mid_ref, right_ref, in_ref, late_ref, early_end_ref, end_ref, state_ref):
    @pl.when(pl.program_id(0) == 0)
    def _():
        state_ref[...] = jnp.zeros_like(state_ref)

    states = [state_ref[0], state_ref[1]]
    for j in range(feat_ref.shape[1]):
        row = pl.ds(j, 1)
        for half in range(2):
            push = in_ref[half, row, :] * feat_ref[half, j].astype(jnp.float32)
            states[half] = (
                stencil(states[half], left_ref[half, row, :], mid_ref[half, row, :], right_ref[half, row, :]) + push
            )
    state_ref[0] = states[0]
    state_ref[1] = states[1]

    @pl.when(pl.program_id(0) == pl.num_programs(0) - 1)
    def _():
        early_end_ref[...] = states[0]
        end_ref[...] = states[1] + jnp.dot(
            states[0], late_ref[...], precision=HIGHEST, preferred_element_type=jnp.float32
        )


def ending(features, coefs, late):
    _, rows, channels, width = features.shape
    coef_spec = pl.BlockSpec((2, STEP_ROWS, width), lambda i: (0, i, 0))
    state = jax.ShapeDtypeStruct((channels, width), jnp.float32)
    state_spec = pl.BlockSpec((channels, width), lambda i: (0, 0))
    return pl.pallas_call(
        ending_kernel,
        grid=(rows // STEP_ROWS,),
        in_specs=[pl.BlockSpec((2, STEP_ROWS, channels, width), lambda i: (0, i, 0, 0))]
        + [coef_spec] * 4
        + [pl.BlockSpec((width, width), lambda i: (0, 0))],
        out_specs=(state_spec, state_spec),
        out_shape=(state, state),
        scratch_shapes=[pltpu.VMEM((2, channels, width), jnp.float32)],
        cost_estimate=pl.CostEstimate(
            flops=14 * rows * channels * width, bytes_accessed=4 * rows * channels * width, transcendentals=0
        ),
        compiler_params=pltpu.CompilerParams(vmem_limit_bytes=VMEM_LIMIT),
        name="ending",
    )(features, *coefs, late)


def applied(state, operator):
    high = state.astype(jnp.bfloat16)
    low = (state - high.astype(jnp.float32)).astype(jnp.bfloat16)
    both = jnp.dot(jnp.concatenate([high, low]), operator, preferred_element_type=jnp.float32)
    return both[: state.shape[0]] + both[state.shape[0] :]


def gated_kernel(
    core_ref, comp_1_ref, comp_2_ref, chip_1_ref, chip_2_ref, chip_3_ref, their_op_ref, their_end_ref,
    early_ref, early_end_ref, feat_ref, gate_ref, left_ref, mid_ref, right_ref, in_ref, out_ref, state_ref,
):
    @pl.when(pl.program_id(0) == 0)
    def _():
        incoming = applied(chip_3_ref[...], comp_2_ref[...]) + chip_2_ref[...]
        incoming = applied(incoming, comp_1_ref[...]) + chip_1_ref[...]
        later = applied(incoming, their_op_ref[...]) + their_end_ref[...]
        incoming = jnp.where(core_ref[0] == 0, incoming, later)
        state_ref[0] = incoming
        state_ref[1] = early_end_ref[...] + jnp.dot(
            incoming, early_ref[...], precision=HIGHEST, preferred_element_type=jnp.float32
        )

    states = [state_ref[0], state_ref[1]]
    for j in range(feat_ref.shape[1]):
        row = pl.ds(j, 1)
        for half in range(2):
            push = in_ref[half, row, :] * feat_ref[half, j].astype(jnp.float32)
            states[half] = (
                stencil(states[half], left_ref[half, row, :], mid_ref[half, row, :], right_ref[half, row, :]) + push
            )
            gate = gate_ref[half, j].astype(jnp.float32)
            out_ref[half, j] = (states[half] * (gate / (1.0 + jnp.exp(-gate)))).astype(out_ref.dtype)
    state_ref[0] = states[0]
    state_ref[1] = states[1]


def gated(core, starts, features, gate_input, coefs):
    _, rows, channels, width = features.shape

    def fixed(array):
        return pl.BlockSpec(array.shape, lambda i, *_: (0,) * array.ndim)

    coef_spec = pl.BlockSpec((2, STEP_ROWS, width), lambda i, *_: (0, i, 0))
    wide_spec = pl.BlockSpec((2, STEP_ROWS, channels, width), lambda i, *_: (0, i, 0, 0))
    return pl.pallas_call(
        gated_kernel,
        grid_spec=pltpu.PrefetchScalarGridSpec(
            num_scalar_prefetch=1,
            grid=(rows // STEP_ROWS,),
            in_specs=[fixed(a) for a in starts] + [wide_spec, wide_spec] + [coef_spec] * 4,
            out_specs=wide_spec,
            scratch_shapes=[pltpu.VMEM((2, channels, width), jnp.float32)],
        ),
        out_shape=jax.ShapeDtypeStruct(features.shape, jnp.bfloat16),
        cost_estimate=pl.CostEstimate(
            flops=24 * rows * channels * width,
            bytes_accessed=12 * rows * channels * width,
            transcendentals=4 * rows * channels * width,
        ),
        compiler_params=pltpu.CompilerParams(vmem_limit_bytes=VMEM_LIMIT),
        name="gated",
    )(core, *starts, features, gate_input, *coefs)


def project_kernel(weight_ref, gated_ref, out_ref, done_ref, sem_ref):
    peers, rows, channels, width = gated_ref.shape
    outs = weight_ref.shape[0]
    tile = outs // TILES
    copies = []
    for row in range(rows):
        here = gated_ref[:, row].reshape(peers * channels, width)
        for t in range(TILES):
            part = pl.ds(t * tile, tile)
            done_ref[row, part, :] = jnp.dot(
                weight_ref[part, :], here, preferred_element_type=jnp.float32
            ).astype(done_ref.dtype)
            copy = pltpu.make_async_copy(done_ref.at[row, part], out_ref.at[row, part], sem_ref.at[row, t])
            copy.start()
            copies.append(copy)
    for copy in copies:
        copy.wait()


def project(out_weight, gathered):
    _, rows, _, width = gathered.shape
    outs = out_weight.shape[0]
    return pl.pallas_call(
        project_kernel,
        in_specs=[pl.BlockSpec(memory_space=pltpu.VMEM)] * 2,
        out_specs=pl.BlockSpec(memory_space=pl.ANY),
        out_shape=jax.ShapeDtypeStruct((rows, outs, width), jnp.bfloat16),
        scratch_shapes=[
            pltpu.VMEM((rows, outs, width), jnp.bfloat16),
            pltpu.SemaphoreType.DMA((rows, TILES)),
        ],
        compiler_params=pltpu.CompilerParams(vmem_limit_bytes=VMEM_LIMIT),
        cost_estimate=pl.CostEstimate(
            flops=2 * rows * outs * outs * width, bytes_accessed=4 * outs * outs, transcendentals=0
        ),
        name="project",
    )(out_weight, gathered)


def shards(slabs, peers, features, mixing, decay_rate, gate_input, out_weight):
    rows, channels, width = features.shape
    features = features.reshape(2, rows // 2, channels, width)
    gate_input = gate_input.reshape(2, rows // 2, channels, width)
    core = lax.axis_index("rows") % 2
    first = core == 0

    def chips_back(value, shift, chip):
        return lax.ppermute(value, "rows", [(i, i + 2 * shift) for i in range(2 * chip, slabs - 2 * shift)])

    def swapped(value):
        return lax.ppermute(value, "rows", [(i, i ^ 1) for i in range(slabs)])

    def in_order(mine, theirs):
        return jnp.where(first, mine, theirs), jnp.where(first, theirs, mine)

    operator, early, late, *coefs = operator_of(mixing, decay_rate)
    coefs = [c.reshape(2, rows // 2, width) for c in coefs]
    their_op = swapped(operator)
    op_0, op_1 = in_order(operator, their_op)
    composite = jnp.dot(op_0, op_1, preferred_element_type=jnp.float32).astype(jnp.bfloat16)
    comp_2 = chips_back(composite, 2, 1)
    comp_1 = chips_back(composite, 1, 1)
    early_end, end = ending(features, coefs, late)
    their_end = swapped(end)
    end_0, end_1 = in_order(end, their_end)
    chip_end = applied(end_0, op_1) + end_1
    chip_3, chip_2, chip_1 = [chips_back(chip_end, shift, 0) for shift in (3, 2, 1)]

    starts = (comp_1, comp_2, chip_1, chip_2, chip_3, their_op, their_end, early, early_end)
    mixed = gated(core.astype(jnp.int32).reshape(1), starts, features, gate_input, coefs)
    mixed = mixed.reshape(peers, rows // peers, channels, width)
    return project(out_weight, lax.all_to_all(mixed, "chan", split_axis=0, concat_axis=0, tiled=True))


def solution(mesh):
    in_specs = (
        P("rows", "chan", None),
        P(None, "rows", None),
        P("rows", None),
        P("rows", "chan", None),
        P(),
    )
    out_specs = P(("rows", "chan"), None, None)

    def whole(features, mixing, decay_rate, gate_input, out_weight):
        return shards(
            mesh.shape["rows"], mesh.shape["chan"], features, mixing, decay_rate, gate_input, out_weight
        )

    return jax.shard_map(whole, mesh=mesh, in_specs=in_specs, out_specs=out_specs, check_vma=False)
```

```python
import jax
import jax.numpy as jnp
from jax import lax
from jax.experimental import pallas as pl
from jax.experimental.pallas import tpu as pltpu
from jax.sharding import PartitionSpec as P

STEP_ROWS = 8
BLOCK = 8
SUBLANES = 8
LANES = 128
TILES = 4
VMEM_LIMIT = 16 * 1024 * 1024


def stencil(state, left_w, mid_w, right_w):
    width = state.shape[1]
    before_col = pltpu.roll(state, 1, 1)
    after_col = pltpu.roll(state, width - 1, 1)
    return left_w * before_col + mid_w * state + right_w * after_col


def split(value):
    high = value.astype(jnp.bfloat16)
    return high, (value - high.astype(jnp.float32)).astype(jnp.bfloat16)


def product(left, right):
    (left_high, left_low), (right_high, right_low) = left, right
    out = jnp.dot(left_high, right_high, preferred_element_type=jnp.float32)
    out = out + jnp.dot(left_high, right_low, preferred_element_type=jnp.float32)
    return out + jnp.dot(left_low, right_high, preferred_element_type=jnp.float32)


def operator_kernel(
    mix_ref, decay_ref, op_ref, early_ref, late_ref, left_ref, mid_ref, right_ref, in_ref,
    side_ref, diag_ref, dense_ref,
):
    rows, width = decay_ref.shape
    decay = decay_ref[...]
    retain = 1.0 - decay
    for side, ref in enumerate((left_ref, mid_ref, right_ref)):
        value = retain * mix_ref[side]
        ref[...] = value
        for part in range(width // LANES):
            side_ref[side, part] = value[:, part * LANES : (part + 1) * LANES]
    in_ref[...] = jnp.sqrt(decay)

    blocks = rows // BLOCK

    def weights(j):
        row = pl.ds(j, blocks, stride=BLOCK)
        return [
            jnp.concatenate([side_ref[side, part, row, :] for part in range(width // LANES)], axis=1)
            for side in range(3)
        ]

    left_w, mid_w, right_w = weights(0)
    diagonals = {-1: left_w, 0: mid_w, 1: right_w}
    for j in range(1, BLOCK):
        left_w, mid_w, right_w = weights(j)
        news = {}
        for d, values in diagonals.items():
            terms = (
                (d - 1, left_w * pltpu.roll(values, 1, 1)),
                (d, mid_w * values),
                (d + 1, right_w * pltpu.roll(values, width - 1, 1)),
            )
            for to, term in terms:
                news[to] = news[to] + term if to in news else term
        diagonals = news
    for d, values in diagonals.items():
        diag_ref[d + BLOCK] = values

    lead = lax.broadcasted_iota(jnp.int32, (SUBLANES, LANES), 1) - lax.broadcasted_iota(
        jnp.int32, (SUBLANES, LANES), 0
    )
    for left in range(0, width, LANES):
        lanes = slice(left, left + LANES)
        low = max(0, left - SUBLANES)
        high = min(width, left + LANES + SUBLANES)
        for b in range(blocks):
            if low > 0:
                dense_ref[b, 0:low, lanes] = jnp.zeros((low, LANES), jnp.float32)
            if high < width:
                dense_ref[b, high:width, lanes] = jnp.zeros((width - high, LANES), jnp.float32)
        for top in range(low, high, SUBLANES):
            tiles = [jnp.zeros((SUBLANES, LANES), jnp.float32)] * blocks
            for d in range(-BLOCK, BLOCK + 1):
                offset = top - d - left
                if -SUBLANES < offset < LANES:
                    here = lead == offset
                    for b in range(blocks):
                        row = jnp.broadcast_to(diag_ref[d + BLOCK, b : b + 1, lanes], (SUBLANES, LANES))
                        tiles[b] = jnp.where(here, row, tiles[b])
            for b in range(blocks):
                dense_ref[b, top : top + SUBLANES, lanes] = tiles[b]

    pairs = [split(product(split(dense_ref[b]), split(dense_ref[b + 1]))) for b in range(0, blocks, 2)]
    early = split(product(pairs[0], pairs[1]))
    late = split(product(pairs[2], pairs[3]))
    for out, value in ((early_ref, early), (late_ref, late)):
        out[0] = value[0]
        out[1] = value[1]
    op_ref[...] = product(early, late).astype(op_ref.dtype)


def operator_of(mixing, decay_rate):
    _, rows, width = mixing.shape
    halves = jax.ShapeDtypeStruct((2, width, width), jnp.bfloat16)
    coef = jax.ShapeDtypeStruct((rows, width), jnp.float32)
    return pl.pallas_call(
        operator_kernel,
        out_shape=(jax.ShapeDtypeStruct((width, width), jnp.bfloat16), halves, halves, coef, coef, coef, coef),
        scratch_shapes=[
            pltpu.VMEM((3, width // LANES, rows, LANES), jnp.float32),
            pltpu.VMEM((2 * BLOCK + 1, rows // BLOCK, width), jnp.float32),
            pltpu.VMEM((rows // BLOCK, width, width), jnp.float32),
        ],
        cost_estimate=pl.CostEstimate(
            flops=5 * rows * width * width, bytes_accessed=8 * rows * width * 4, transcendentals=0
        ),
        compiler_params=pltpu.CompilerParams(vmem_limit_bytes=VMEM_LIMIT),
        name="operator",
    )(mixing, decay_rate)


def ending_kernel(feat_ref, left_ref, mid_ref, right_ref, in_ref, late_ref, early_end_ref, end_ref, state_ref):
    @pl.when(pl.program_id(0) == 0)
    def _():
        state_ref[...] = jnp.zeros_like(state_ref)

    states = [state_ref[0], state_ref[1]]
    for j in range(feat_ref.shape[1]):
        row = pl.ds(j, 1)
        for half in range(2):
            push = in_ref[half, row, :] * feat_ref[half, j].astype(jnp.float32)
            states[half] = (
                stencil(states[half], left_ref[half, row, :], mid_ref[half, row, :], right_ref[half, row, :]) + push
            )
    state_ref[0] = states[0]
    state_ref[1] = states[1]

    @pl.when(pl.program_id(0) == pl.num_programs(0) - 1)
    def _():
        early_end_ref[...] = states[0]
        end_ref[...] = states[1] + product(split(states[0]), (late_ref[0], late_ref[1]))


def ending(features, coefs, late):
    _, rows, channels, width = features.shape
    coef_spec = pl.BlockSpec((2, STEP_ROWS, width), lambda i: (0, i, 0))
    state = jax.ShapeDtypeStruct((channels, width), jnp.float32)
    state_spec = pl.BlockSpec((channels, width), lambda i: (0, 0))
    return pl.pallas_call(
        ending_kernel,
        grid=(rows // STEP_ROWS,),
        in_specs=[pl.BlockSpec((2, STEP_ROWS, channels, width), lambda i: (0, i, 0, 0))]
        + [coef_spec] * 4
        + [pl.BlockSpec((2, width, width), lambda i: (0, 0, 0))],
        out_specs=(state_spec, state_spec),
        out_shape=(state, state),
        scratch_shapes=[pltpu.VMEM((2, channels, width), jnp.float32)],
        cost_estimate=pl.CostEstimate(
            flops=14 * rows * channels * width, bytes_accessed=4 * rows * channels * width, transcendentals=0
        ),
        compiler_params=pltpu.CompilerParams(vmem_limit_bytes=VMEM_LIMIT),
        name="ending",
    )(features, *coefs, late)


def applied(state, operator):
    both = jnp.dot(jnp.concatenate(split(state)), operator, preferred_element_type=jnp.float32)
    return both[: state.shape[0]] + both[state.shape[0] :]


def gated_kernel(
    core_ref, hop_1_ref, hop_2_ref, hop_3_ref, their_op_ref, their_end_ref, early_ref, early_end_ref,
    feat_ref, gate_ref, left_ref, mid_ref, right_ref, in_ref, out_ref, state_ref,
):
    @pl.when(pl.program_id(0) == 0)
    def _():
        incoming = hop_1_ref[...] + hop_2_ref[...] + hop_3_ref[...]
        later = applied(incoming, their_op_ref[...]) + their_end_ref[...]
        incoming = jnp.where(core_ref[0] == 0, incoming, later)
        state_ref[0] = incoming
        state_ref[1] = early_end_ref[...] + product(split(incoming), (early_ref[0], early_ref[1]))

    states = [state_ref[0], state_ref[1]]
    for j in range(feat_ref.shape[1]):
        row = pl.ds(j, 1)
        for half in range(2):
            push = in_ref[half, row, :] * feat_ref[half, j].astype(jnp.float32)
            states[half] = (
                stencil(states[half], left_ref[half, row, :], mid_ref[half, row, :], right_ref[half, row, :]) + push
            )
            gate = gate_ref[half, j].astype(jnp.float32)
            out_ref[half, j] = (states[half] * (gate / (1.0 + jnp.exp(-gate)))).astype(out_ref.dtype)
    state_ref[0] = states[0]
    state_ref[1] = states[1]


def gated(core, starts, features, gate_input, coefs):
    _, rows, channels, width = features.shape

    def fixed(array):
        return pl.BlockSpec(array.shape, lambda i, *_: (0,) * array.ndim)

    coef_spec = pl.BlockSpec((2, STEP_ROWS, width), lambda i, *_: (0, i, 0))
    wide_spec = pl.BlockSpec((2, STEP_ROWS, channels, width), lambda i, *_: (0, i, 0, 0))
    return pl.pallas_call(
        gated_kernel,
        grid_spec=pltpu.PrefetchScalarGridSpec(
            num_scalar_prefetch=1,
            grid=(rows // STEP_ROWS,),
            in_specs=[fixed(a) for a in starts] + [wide_spec, wide_spec] + [coef_spec] * 4,
            out_specs=wide_spec,
            scratch_shapes=[pltpu.VMEM((2, channels, width), jnp.float32)],
        ),
        out_shape=jax.ShapeDtypeStruct(features.shape, jnp.bfloat16),
        cost_estimate=pl.CostEstimate(
            flops=24 * rows * channels * width,
            bytes_accessed=12 * rows * channels * width,
            transcendentals=4 * rows * channels * width,
        ),
        compiler_params=pltpu.CompilerParams(vmem_limit_bytes=VMEM_LIMIT),
        name="gated",
    )(core, *starts, features, gate_input, *coefs)


def project_kernel(weight_ref, gated_ref, out_ref, done_ref, sem_ref):
    peers, rows, channels, width = gated_ref.shape
    outs = weight_ref.shape[0]
    tile = outs // TILES
    copies = []
    for row in range(rows):
        here = gated_ref[:, row].reshape(peers * channels, width)
        for t in range(TILES):
            part = pl.ds(t * tile, tile)
            done_ref[row, part, :] = jnp.dot(
                weight_ref[part, :], here, preferred_element_type=jnp.float32
            ).astype(done_ref.dtype)
            copy = pltpu.make_async_copy(done_ref.at[row, part], out_ref.at[row, part], sem_ref.at[row, t])
            copy.start()
            copies.append(copy)
    for copy in copies:
        copy.wait()


def project(out_weight, gathered):
    _, rows, _, width = gathered.shape
    outs = out_weight.shape[0]
    return pl.pallas_call(
        project_kernel,
        in_specs=[pl.BlockSpec(memory_space=pltpu.VMEM)] * 2,
        out_specs=pl.BlockSpec(memory_space=pl.ANY),
        out_shape=jax.ShapeDtypeStruct((rows, outs, width), jnp.bfloat16),
        scratch_shapes=[
            pltpu.VMEM((rows, outs, width), jnp.bfloat16),
            pltpu.SemaphoreType.DMA((rows, TILES)),
        ],
        compiler_params=pltpu.CompilerParams(vmem_limit_bytes=VMEM_LIMIT),
        cost_estimate=pl.CostEstimate(
            flops=2 * rows * outs * outs * width, bytes_accessed=4 * outs * outs, transcendentals=0
        ),
        name="project",
    )(out_weight, gathered)


def shards(slabs, peers, features, mixing, decay_rate, gate_input, out_weight):
    rows, channels, width = features.shape
    features = features.reshape(2, rows // 2, channels, width)
    gate_input = gate_input.reshape(2, rows // 2, channels, width)
    core = lax.axis_index("rows") % 2
    first = core == 0

    def hop(value, chip):
        return lax.ppermute(value, "rows", [(2 * chip + c, 2 * chip + 2 + c) for c in range(2)])

    def swapped(value):
        return lax.ppermute(value, "rows", [(i, i ^ 1) for i in range(slabs)])

    def in_order(mine, theirs):
        return jnp.where(first, mine, theirs), jnp.where(first, theirs, mine)

    operator, early, late, *coefs = operator_of(mixing, decay_rate)
    coefs = [c.reshape(2, rows // 2, width) for c in coefs]
    their_op = swapped(operator)
    early_end, end = ending(features, coefs, late)
    their_end = swapped(end)
    op_0, op_1 = in_order(operator, their_op)
    composite = jnp.dot(op_0, op_1, preferred_element_type=jnp.float32).astype(jnp.bfloat16)
    end_0, end_1 = in_order(end, their_end)
    chip_end = applied(end_0, op_1) + end_1
    hops = [hop(chip_end, 0)]
    for chip in range(1, slabs // 2 - 1):
        hops.append(hop(applied(hops[-1], composite) + chip_end, chip))

    starts = (*hops, their_op, their_end, early, early_end)
    mixed = gated(core.astype(jnp.int32).reshape(1), starts, features, gate_input, coefs)
    mixed = mixed.reshape(peers, rows // peers, channels, width)
    return project(out_weight, lax.all_to_all(mixed, "chan", split_axis=0, concat_axis=0, tiled=True))


def solution(mesh):
    in_specs = (
        P("rows", "chan", None),
        P(None, "rows", None),
        P("rows", None),
        P("rows", "chan", None),
        P(),
    )
    out_specs = P(("rows", "chan"), None, None)

    def whole(features, mixing, decay_rate, gate_input, out_weight):
        return shards(
            mesh.shape["rows"], mesh.shape["chan"], features, mixing, decay_rate, gate_input, out_weight
        )

    return jax.shard_map(whole, mesh=mesh, in_specs=in_specs, out_specs=out_specs, check_vma=False)
```

```python
import jax
import jax.numpy as jnp
from jax import lax
from jax.experimental import pallas as pl
from jax.experimental.pallas import tpu as pltpu
from jax.sharding import PartitionSpec as P

UNROLL = 8
BLOCK = 8
SUBLANES = 8
LANES = 128
TILES = 4
MIB = 1024 * 1024
SUMMARY_MIB = 62


def stencil(state, left_w, mid_w, right_w):
    width = state.shape[1]
    before_col = pltpu.roll(state, 1, 1)
    after_col = pltpu.roll(state, width - 1, 1)
    return left_w * before_col + mid_w * state + right_w * after_col


def split(value):
    high = value.astype(jnp.bfloat16)
    return high, (value - high.astype(jnp.float32)).astype(jnp.bfloat16)


def product(left, right):
    (left_high, left_low), (right_high, right_low) = left, right
    out = jnp.dot(left_high, right_high, preferred_element_type=jnp.float32)
    out = out + jnp.dot(left_high, right_low, preferred_element_type=jnp.float32)
    return out + jnp.dot(left_low, right_high, preferred_element_type=jnp.float32)


def sweep(states, feat_ref, keep_ref, rows, take=None):
    def step(i, states):
        news = []
        for half in range(2):
            left_w, mid_w, right_w, in_w = [
                keep_ref[pl.ds(i + half * rows + k * 2 * rows, 1), :] for k in range(4)
            ]
            push = in_w * feat_ref[i + half * rows].astype(jnp.float32)
            news.append(stencil(states[half], left_w, mid_w, right_w) + push)
            if take is not None:
                take(i + half * rows, news[half])
        return tuple(news)

    return lax.fori_loop(0, rows, step, states, unroll=UNROLL)


def summary_kernel(
    mix_hbm, decay_hbm, feat_hbm, pack_ref, keep_ref,
    mix_ref, decay_ref, feat_ref, sem_ref, side_ref, diag_ref, dense_ref,
):
    copies = [
        pltpu.make_async_copy(source, target, sem_ref.at[k])
        for k, (source, target) in enumerate(
            ((mix_hbm, mix_ref), (decay_hbm, decay_ref), (feat_hbm, feat_ref))
        )
    ]
    for copy in copies:
        copy.start()
    copies[0].wait()
    copies[1].wait()
    rows, width = decay_ref.shape
    decay = decay_ref[...]
    retain = 1.0 - decay
    for side in range(3):
        value = retain * mix_ref[side]
        keep_ref[side * rows : (side + 1) * rows] = value
        for part in range(width // LANES):
            side_ref[side, part] = value[:, part * LANES : (part + 1) * LANES]
    keep_ref[3 * rows : 4 * rows] = jnp.sqrt(decay)

    blocks = rows // BLOCK

    def weights(j):
        row = pl.ds(j, blocks, stride=BLOCK)
        return [
            jnp.concatenate([side_ref[side, part, row, :] for part in range(width // LANES)], axis=1)
            for side in range(3)
        ]

    left_w, mid_w, right_w = weights(0)
    diagonals = {-1: left_w, 0: mid_w, 1: right_w}
    for j in range(1, BLOCK):
        left_w, mid_w, right_w = weights(j)
        news = {}
        for d, values in diagonals.items():
            terms = (
                (d - 1, left_w * pltpu.roll(values, 1, 1)),
                (d, mid_w * values),
                (d + 1, right_w * pltpu.roll(values, width - 1, 1)),
            )
            for to, term in terms:
                news[to] = news[to] + term if to in news else term
        diagonals = news
    for d, values in diagonals.items():
        diag_ref[d + BLOCK] = values

    lead = lax.broadcasted_iota(jnp.int32, (SUBLANES, LANES), 1) - lax.broadcasted_iota(
        jnp.int32, (SUBLANES, LANES), 0
    )
    for left in range(0, width, LANES):
        lanes = slice(left, left + LANES)
        low = max(0, left - SUBLANES)
        high = min(width, left + LANES + SUBLANES)
        for b in range(blocks):
            if low > 0:
                dense_ref[b, 0:low, lanes] = jnp.zeros((low, LANES), jnp.float32)
            if high < width:
                dense_ref[b, high:width, lanes] = jnp.zeros((width - high, LANES), jnp.float32)
        for top in range(low, high, SUBLANES):
            tiles = [jnp.zeros((SUBLANES, LANES), jnp.float32)] * blocks
            for d in range(-BLOCK, BLOCK + 1):
                offset = top - d - left
                if -SUBLANES < offset < LANES:
                    here = lead == offset
                    for b in range(blocks):
                        row = jnp.broadcast_to(diag_ref[d + BLOCK, b : b + 1, lanes], (SUBLANES, LANES))
                        tiles[b] = jnp.where(here, row, tiles[b])
            for b in range(blocks):
                dense_ref[b, top : top + SUBLANES, lanes] = tiles[b]

    pairs = [split(product(split(dense_ref[b]), split(dense_ref[b + 1]))) for b in range(0, blocks, 2)]
    early = product(pairs[0], pairs[1])
    keep_ref[4 * rows : 4 * rows + width] = early
    early = split(early)
    late = split(product(pairs[2], pairs[3]))
    pack_ref[0:width] = product(early, late).astype(pack_ref.dtype)

    copies[2].wait()
    channels = feat_ref.shape[1]
    zero = jnp.zeros((channels, width), jnp.float32)
    first, second = sweep((zero, zero), feat_ref, keep_ref, rows // 2)
    keep_ref[4 * rows + width : 4 * rows + width + channels] = first
    high, low = split(second + product(split(first), late))
    pack_ref[width : width + channels] = high
    pack_ref[width + channels : width + 2 * channels] = low


def summary(features, mixing, decay_rate):
    rows, channels, width = features.shape
    vmem = pl.BlockSpec(memory_space=pltpu.VMEM)
    return pl.pallas_call(
        summary_kernel,
        in_specs=[pl.BlockSpec(memory_space=pltpu.HBM)] * 3,
        out_specs=[vmem] * 2,
        out_shape=(
            jax.ShapeDtypeStruct((width + 2 * channels, width), jnp.bfloat16),
            jax.ShapeDtypeStruct((4 * rows + width + channels, width), jnp.float32),
        ),
        scratch_shapes=[
            pltpu.VMEM(mixing.shape, jnp.float32),
            pltpu.VMEM(decay_rate.shape, jnp.float32),
            pltpu.VMEM(features.shape, features.dtype),
            pltpu.SemaphoreType.DMA((3,)),
            pltpu.VMEM((3, width // LANES, rows, LANES), jnp.float32),
            pltpu.VMEM((2 * BLOCK + 1, rows // BLOCK, width), jnp.float32),
            pltpu.VMEM((rows // BLOCK, width, width), jnp.float32),
        ],
        cost_estimate=pl.CostEstimate(
            flops=14 * rows * channels * width, bytes_accessed=4 * rows * channels * width, transcendentals=0
        ),
        compiler_params=pltpu.CompilerParams(vmem_limit_bytes=SUMMARY_MIB * MIB),
        name="summary",
    )(mixing, decay_rate, features)


def applied(state, operator):
    both = jnp.dot(jnp.concatenate(split(state)), operator, preferred_element_type=jnp.float32)
    return both[: state.shape[0]] + both[state.shape[0] :]


def unpacked(ref, width, channels):
    high = ref[width : width + channels].astype(jnp.float32)
    return high + ref[width + channels : width + 2 * channels].astype(jnp.float32)


def gated_kernel(core_ref, *refs):
    hop_refs, refs = refs[:3], refs[3:]
    theirs_ref, keep_ref, feat_ref, gate_ref, out_ref = refs
    rows, channels, width = feat_ref.shape
    incoming = hop_refs[0][...] + hop_refs[1][...] + hop_refs[2][...]
    later = applied(incoming, theirs_ref[0:width]) + unpacked(theirs_ref, width, channels)
    incoming = jnp.where(core_ref[0] == 0, incoming, later)
    early = keep_ref[4 * rows : 4 * rows + width]
    second = keep_ref[4 * rows + width : 4 * rows + width + channels] + product(split(incoming), split(early))

    def take(row, state):
        gate = gate_ref[row].astype(jnp.float32)
        out_ref[row] = (state * (gate / (1.0 + jnp.exp(-gate)))).astype(out_ref.dtype)

    sweep((incoming, second), feat_ref, keep_ref, rows // 2, take)


def gated(core, starts, features, gate_input):
    rows, channels, width = features.shape
    vmem = pl.BlockSpec(memory_space=pltpu.VMEM)
    return pl.pallas_call(
        gated_kernel,
        in_specs=[pl.BlockSpec(memory_space=pltpu.SMEM)] + [vmem] * (len(starts) + 2),
        out_specs=vmem,
        out_shape=jax.ShapeDtypeStruct(features.shape, jnp.bfloat16),
        cost_estimate=pl.CostEstimate(
            flops=48 * rows * channels * width,
            bytes_accessed=24 * rows * channels * width,
            transcendentals=8 * rows * channels * width,
        ),
        compiler_params=pltpu.CompilerParams(vmem_limit_bytes=8 * MIB),
        name="gated",
    )(core, *starts, features, gate_input)


def project_kernel(weight_ref, gated_ref, out_ref, done_ref, sem_ref):
    peers, rows, channels, width = gated_ref.shape
    outs = weight_ref.shape[0]
    tile = outs // TILES
    copies = []
    for row in range(rows):
        here = gated_ref[:, row].reshape(peers * channels, width)
        for t in range(TILES):
            part = pl.ds(t * tile, tile)
            done_ref[row, part, :] = jnp.dot(
                weight_ref[part, :], here, preferred_element_type=jnp.float32
            ).astype(done_ref.dtype)
            copy = pltpu.make_async_copy(done_ref.at[row, part], out_ref.at[row, part], sem_ref.at[row, t])
            copy.start()
            copies.append(copy)
    for copy in copies:
        copy.wait()


def project(out_weight, gathered):
    _, rows, _, width = gathered.shape
    outs = out_weight.shape[0]
    return pl.pallas_call(
        project_kernel,
        in_specs=[pl.BlockSpec(memory_space=pltpu.VMEM)] * 2,
        out_specs=pl.BlockSpec(memory_space=pl.ANY),
        out_shape=jax.ShapeDtypeStruct((rows, outs, width), jnp.bfloat16),
        scratch_shapes=[
            pltpu.VMEM((rows, outs, width), jnp.bfloat16),
            pltpu.SemaphoreType.DMA((rows, TILES)),
        ],
        compiler_params=pltpu.CompilerParams(vmem_limit_bytes=8 * MIB),
        cost_estimate=pl.CostEstimate(
            flops=2 * rows * outs * outs * width, bytes_accessed=4 * outs * outs, transcendentals=0
        ),
        name="project",
    )(out_weight, gathered)


def shards(slabs, peers, features, mixing, decay_rate, gate_input, out_weight):
    rows, channels, width = features.shape
    core = lax.axis_index("rows") % 2
    first = core == 0

    def chip_to(value, *pairs):
        return lax.ppermute(value, "rows", [(2 * a + c, 2 * b + c) for a, b in pairs for c in range(2)])

    mine, keep = summary(features, mixing, decay_rate)
    theirs = lax.ppermute(mine, "rows", [(i, i ^ 1) for i in range(slabs)])
    earlier = jnp.where(first, mine, theirs)
    later = jnp.where(first, theirs, mine)
    op_0, op_1 = earlier[:width], later[:width]
    chip_end = applied(unpacked(earlier, width, channels), op_1) + unpacked(later, width, channels)
    composite = jnp.dot(op_0, op_1, preferred_element_type=jnp.float32).astype(jnp.bfloat16)
    before = chip_to(chip_end, (0, 1), (1, 2), (2, 3))
    operator_on = chip_to(composite, (2, 3))
    carried = applied(before, composite) + chip_end
    far = chip_to(carried, (1, 3))
    near = chip_to(carried, (1, 2))
    chip = lax.axis_index("rows") // 2
    last = applied(far, operator_on) + before
    zero = jnp.zeros_like(last)
    hops = (jnp.where(chip == 1, before, zero), near, jnp.where(chip == 3, last, zero))

    starts = (*hops, theirs, keep)
    mixed = gated(core.astype(jnp.int32).reshape(1), starts, features, gate_input)
    mixed = mixed.reshape(peers, rows // peers, channels, width)
    return project(out_weight, lax.all_to_all(mixed, "chan", split_axis=0, concat_axis=0, tiled=True))


def solution(mesh):
    in_specs = (
        P("rows", "chan", None),
        P(None, "rows", None),
        P("rows", None),
        P("rows", "chan", None),
        P(),
    )
    out_specs = P(("rows", "chan"), None, None)

    def whole(features, mixing, decay_rate, gate_input, out_weight):
        return shards(
            mesh.shape["rows"], mesh.shape["chan"], features, mixing, decay_rate, gate_input, out_weight
        )

    return jax.shard_map(whole, mesh=mesh, in_specs=in_specs, out_specs=out_specs, check_vma=False)
```

```python
import jax
import jax.numpy as jnp
from jax import lax
from jax.experimental import pallas as pl
from jax.experimental.pallas import tpu as pltpu
from jax.sharding import PartitionSpec as P

UNROLL = 8
BLOCK = 8
SUBLANES = 8
LANES = 128
TILES = 4
MIB = 1024 * 1024


def stencil(state, left_w, mid_w, right_w):
    width = state.shape[1]
    before_col = pltpu.roll(state, 1, 1)
    after_col = pltpu.roll(state, width - 1, 1)
    return left_w * before_col + mid_w * state + right_w * after_col


def split(value):
    high = value.astype(jnp.bfloat16)
    return high, (value - high.astype(jnp.float32)).astype(jnp.bfloat16)


def product(left, right):
    (left_high, left_low), (right_high, right_low) = left, right
    out = jnp.dot(left_high, right_high, preferred_element_type=jnp.float32)
    out = out + jnp.dot(left_high, right_low, preferred_element_type=jnp.float32)
    return out + jnp.dot(left_low, right_high, preferred_element_type=jnp.float32)


def sweep(states, feat_ref, keep_ref, rows, take=None):
    def step(i, states):
        news = []
        for half in range(2):
            left_w, mid_w, right_w, in_w = [
                keep_ref[pl.ds(i + half * rows + k * 2 * rows, 1), :] for k in range(4)
            ]
            push = in_w * feat_ref[i + half * rows].astype(jnp.float32)
            news.append(stencil(states[half], left_w, mid_w, right_w) + push)
            if take is not None:
                take(i + half * rows, news[half])
        return tuple(news)

    return lax.fori_loop(0, rows, step, states, unroll=UNROLL)


def summary_kernel(
    _, mix_hbm, decay_hbm, feat_hbm, gate_hbm, pack_ref, keep_ref, feat_ref, gate_ref,
    mix_ref, decay_ref, sem_ref, side_ref, diag_ref, dense_ref,
):
    copies = [
        pltpu.make_async_copy(source, target, sem_ref.at[k])
        for k, (source, target) in enumerate(
            ((mix_hbm, mix_ref), (decay_hbm, decay_ref), (feat_hbm, feat_ref), (gate_hbm, gate_ref))
        )
    ]
    for copy in copies:
        copy.start()
    copies[0].wait()
    copies[1].wait()
    rows, width = decay_ref.shape
    decay = decay_ref[...]
    retain = 1.0 - decay
    for side in range(3):
        value = retain * mix_ref[side]
        keep_ref[side * rows : (side + 1) * rows] = value
        for part in range(width // LANES):
            side_ref[side, part] = value[:, part * LANES : (part + 1) * LANES]
    keep_ref[3 * rows : 4 * rows] = jnp.sqrt(decay)

    blocks = rows // BLOCK

    def weights(j):
        row = pl.ds(j, blocks, stride=BLOCK)
        return [
            jnp.concatenate([side_ref[side, part, row, :] for part in range(width // LANES)], axis=1)
            for side in range(3)
        ]

    left_w, mid_w, right_w = weights(0)
    diagonals = {-1: left_w, 0: mid_w, 1: right_w}
    for j in range(1, BLOCK):
        left_w, mid_w, right_w = weights(j)
        news = {}
        for d, values in diagonals.items():
            terms = (
                (d - 1, left_w * pltpu.roll(values, 1, 1)),
                (d, mid_w * values),
                (d + 1, right_w * pltpu.roll(values, width - 1, 1)),
            )
            for to, term in terms:
                news[to] = news[to] + term if to in news else term
        diagonals = news
    for d, values in diagonals.items():
        diag_ref[d + BLOCK] = values

    lead = lax.broadcasted_iota(jnp.int32, (SUBLANES, LANES), 1) - lax.broadcasted_iota(
        jnp.int32, (SUBLANES, LANES), 0
    )
    for left in range(0, width, LANES):
        lanes = slice(left, left + LANES)
        low = max(0, left - SUBLANES)
        high = min(width, left + LANES + SUBLANES)
        for b in range(blocks):
            if low > 0:
                dense_ref[b, 0:low, lanes] = jnp.zeros((low, LANES), jnp.float32)
            if high < width:
                dense_ref[b, high:width, lanes] = jnp.zeros((width - high, LANES), jnp.float32)
        for top in range(low, high, SUBLANES):
            tiles = [jnp.zeros((SUBLANES, LANES), jnp.float32)] * blocks
            for d in range(-BLOCK, BLOCK + 1):
                offset = top - d - left
                if -SUBLANES < offset < LANES:
                    here = lead == offset
                    for b in range(blocks):
                        row = jnp.broadcast_to(diag_ref[d + BLOCK, b : b + 1, lanes], (SUBLANES, LANES))
                        tiles[b] = jnp.where(here, row, tiles[b])
            for b in range(blocks):
                dense_ref[b, top : top + SUBLANES, lanes] = tiles[b]

    pairs = [split(product(split(dense_ref[b]), split(dense_ref[b + 1]))) for b in range(0, blocks, 2)]
    early = product(pairs[0], pairs[1])
    keep_ref[4 * rows : 4 * rows + width] = early
    early = split(early)
    late = split(product(pairs[2], pairs[3]))
    pack_ref[0:width] = product(early, late).astype(pack_ref.dtype)

    copies[2].wait()
    channels = feat_ref.shape[1]
    zero = jnp.zeros((channels, width), jnp.float32)
    first, second = sweep((zero, zero), feat_ref, keep_ref, rows // 2)
    keep_ref[4 * rows + width : 4 * rows + width + channels] = first
    high, low = split(second + product(split(first), late))
    pack_ref[width : width + channels] = high
    pack_ref[width + channels : width + 2 * channels] = low
    copies[3].wait()


def summary(place, features, gate_input, mixing, decay_rate):
    rows, channels, width = features.shape
    vmem = pl.BlockSpec(memory_space=pltpu.VMEM)
    return pl.pallas_call(
        summary_kernel,
        in_specs=[pl.BlockSpec(memory_space=pltpu.SMEM)] + [pl.BlockSpec(memory_space=pltpu.HBM)] * 4,
        out_specs=[vmem] * 4,
        out_shape=(
            pltpu.VMEM((width + 2 * channels, width), jnp.bfloat16),
            pltpu.VMEM((4 * rows + width + channels, width), jnp.float32),
            pltpu.VMEM(features.shape, features.dtype),
            pltpu.VMEM(gate_input.shape, gate_input.dtype),
        ),
        scratch_shapes=[
            pltpu.VMEM(mixing.shape, jnp.float32),
            pltpu.VMEM(decay_rate.shape, jnp.float32),
            pltpu.SemaphoreType.DMA((4,)),
            pltpu.VMEM((3, width // LANES, rows, LANES), jnp.float32),
            pltpu.VMEM((2 * BLOCK + 1, rows // BLOCK, width), jnp.float32),
            pltpu.VMEM((rows // BLOCK, width, width), jnp.float32),
        ],
        cost_estimate=pl.CostEstimate(
            flops=14 * rows * channels * width, bytes_accessed=26 * MIB, transcendentals=0
        ),
        compiler_params=pltpu.CompilerParams(vmem_limit_bytes=16 * MIB),
        name="summary",
    )(place, *[pltpu.with_memory_space_constraint(a, pltpu.HBM) for a in (mixing, decay_rate, features, gate_input)])


def applied(state, operator):
    both = jnp.dot(jnp.concatenate(split(state)), operator, preferred_element_type=jnp.float32)
    return both[: state.shape[0]] + both[state.shape[0] :]


def unpacked(ref, width, channels):
    high = ref[width : width + channels].astype(jnp.float32)
    return high + ref[width + channels : width + 2 * channels].astype(jnp.float32)


def chip_kernel(place_ref, mine_ref, theirs_ref, on_ref, end_ref):
    channels, width = end_ref.shape

    def write(earlier_ref, later_ref):
        later_op = later_ref[0:width]
        end = applied(unpacked(earlier_ref, width, channels), later_op) + unpacked(later_ref, width, channels)
        end_ref[...] = end
        high, low = split(end)
        on_ref[width : width + channels] = high
        on_ref[width + channels : width + 2 * channels] = low
        both = jnp.dot(earlier_ref[0:width], later_op, preferred_element_type=jnp.float32)
        on_ref[0:width] = both.astype(on_ref.dtype)

    @pl.when(place_ref[0] == 0)
    def _():
        write(mine_ref, theirs_ref)

    @pl.when(place_ref[0] != 0)
    def _():
        write(theirs_ref, mine_ref)


def chip_of(place, mine, theirs):
    width = mine.shape[1]
    channels = (mine.shape[0] - width) // 2
    vmem = pl.BlockSpec(memory_space=pltpu.VMEM)
    return pl.pallas_call(
        chip_kernel,
        in_specs=[pl.BlockSpec(memory_space=pltpu.SMEM), vmem, vmem],
        out_specs=(vmem, vmem),
        out_shape=(
            jax.ShapeDtypeStruct(mine.shape, mine.dtype),
            jax.ShapeDtypeStruct((channels, width), jnp.float32),
        ),
        cost_estimate=pl.CostEstimate(flops=2 * width**3, bytes_accessed=4 * MIB, transcendentals=0),
        compiler_params=pltpu.CompilerParams(vmem_limit_bytes=4 * MIB),
        name="chip",
    )(place, mine, theirs)


def carry_kernel(before_ref, on_ref, end_ref, out_ref):
    out_ref[...] = applied(before_ref[...], on_ref[0 : out_ref.shape[1]]) + end_ref[...]


def carry(before, on, chip_end):
    vmem = pl.BlockSpec(memory_space=pltpu.VMEM)
    return pl.pallas_call(
        carry_kernel,
        in_specs=[vmem] * 3,
        out_specs=vmem,
        out_shape=jax.ShapeDtypeStruct(chip_end.shape, jnp.float32),
        cost_estimate=pl.CostEstimate(flops=2 * on.size, bytes_accessed=2 * MIB, transcendentals=0),
        compiler_params=pltpu.CompilerParams(vmem_limit_bytes=4 * MIB),
        name="carry",
    )(before, on, chip_end)


def gated_kernel(
    place_ref, before_ref, near_ref, far_ref, beyond_ref, theirs_ref, keep_ref, feat_ref, gate_ref, out_ref
):
    rows, channels, width = feat_ref.shape
    farther = applied(far_ref[...], beyond_ref[0:width]) + unpacked(beyond_ref, width, channels)
    incoming = before_ref[...] + near_ref[...] + farther
    later = applied(incoming, theirs_ref[0:width]) + unpacked(theirs_ref, width, channels)
    incoming = jnp.where(place_ref[0] == 0, incoming, later)
    early = keep_ref[4 * rows : 4 * rows + width]
    second = keep_ref[4 * rows + width : 4 * rows + width + channels] + product(split(incoming), split(early))

    def take(row, state):
        gate = gate_ref[row].astype(jnp.float32)
        out_ref[row] = (state * (gate / (1.0 + jnp.exp(-gate)))).astype(out_ref.dtype)

    sweep((incoming, second), feat_ref, keep_ref, rows // 2, take)


def gated(place, starts, features, gate_input):
    rows, channels, width = features.shape
    vmem = pl.BlockSpec(memory_space=pltpu.VMEM)
    return pl.pallas_call(
        gated_kernel,
        in_specs=[pl.BlockSpec(memory_space=pltpu.SMEM)] + [vmem] * (len(starts) + 2),
        out_specs=vmem,
        out_shape=jax.ShapeDtypeStruct(features.shape, jnp.bfloat16),
        cost_estimate=pl.CostEstimate(
            flops=48 * rows * channels * width,
            bytes_accessed=24 * rows * channels * width,
            transcendentals=8 * rows * channels * width,
        ),
        compiler_params=pltpu.CompilerParams(vmem_limit_bytes=8 * MIB),
        name="gated",
    )(place, *starts, features, gate_input)


def project_kernel(weight_ref, gated_ref, out_ref, done_ref, sem_ref):
    peers, rows, channels, width = gated_ref.shape
    outs = weight_ref.shape[0]
    tile = outs // TILES
    copies = []
    for row in range(rows):
        here = gated_ref[:, row].reshape(peers * channels, width)
        for t in range(TILES):
            part = pl.ds(t * tile, tile)
            done_ref[row, part, :] = jnp.dot(
                weight_ref[part, :], here, preferred_element_type=jnp.float32
            ).astype(done_ref.dtype)
            copy = pltpu.make_async_copy(done_ref.at[row, part], out_ref.at[row, part], sem_ref.at[row, t])
            copy.start()
            copies.append(copy)
    for copy in copies:
        copy.wait()


def project(out_weight, gathered):
    _, rows, _, width = gathered.shape
    outs = out_weight.shape[0]
    return pl.pallas_call(
        project_kernel,
        in_specs=[pl.BlockSpec(memory_space=pltpu.VMEM)] * 2,
        out_specs=pl.BlockSpec(memory_space=pl.ANY),
        out_shape=jax.ShapeDtypeStruct((rows, outs, width), jnp.bfloat16),
        scratch_shapes=[
            pltpu.VMEM((rows, outs, width), jnp.bfloat16),
            pltpu.SemaphoreType.DMA((rows, TILES)),
        ],
        compiler_params=pltpu.CompilerParams(vmem_limit_bytes=8 * MIB),
        cost_estimate=pl.CostEstimate(
            flops=2 * rows * outs * outs * width, bytes_accessed=4 * outs * outs, transcendentals=0
        ),
        name="project",
    )(out_weight, gathered)


def shards(slabs, peers, features, mixing, decay_rate, gate_input, out_weight):
    rows, channels, width = features.shape
    place = lax.axis_index("rows").astype(jnp.int32)
    place = jnp.stack([place % 2, place // 2])

    def chip_to(value, *pairs):
        return lax.ppermute(value, "rows", [(2 * a + c, 2 * b + c) for a, b in pairs for c in range(2)])

    mine, keep, features, gate_input = summary(place, features, gate_input, mixing, decay_rate)
    theirs = lax.ppermute(mine, "rows", [(i, i ^ 1) for i in range(slabs)])
    on, chip_end = chip_of(place, mine, theirs)
    before = chip_to(chip_end, (0, 1))
    beyond = chip_to(on, (2, 3))
    carried = carry(before, on, chip_end)
    far = chip_to(carried, (1, 3))
    near = chip_to(carried, (1, 2))

    starts = (before, near, far, beyond, theirs, keep)
    mixed = gated(place, starts, features, gate_input)
    mixed = mixed.reshape(peers, rows // peers, channels, width)
    return project(out_weight, lax.all_to_all(mixed, "chan", split_axis=0, concat_axis=0, tiled=True))


def solution(mesh):
    in_specs = (
        P("rows", "chan", None),
        P(None, "rows", None),
        P("rows", None),
        P("rows", "chan", None),
        P(),
    )
    out_specs = P(("rows", "chan"), None, None)

    def whole(features, mixing, decay_rate, gate_input, out_weight):
        return shards(
            mesh.shape["rows"], mesh.shape["chan"], features, mixing, decay_rate, gate_input, out_weight
        )

    return jax.shard_map(whole, mesh=mesh, in_specs=in_specs, out_specs=out_specs, check_vma=False)
```

```python
import jax
import jax.numpy as jnp
from jax import lax
from jax.experimental import pallas as pl
from jax.experimental.pallas import tpu as pltpu
from jax.sharding import PartitionSpec as P

UNROLL = 8
BLOCK = 8
SUBLANES = 8
LANES = 128
TILES = 4
MIB = 1024 * 1024


def stencil(state, left_w, mid_w, right_w):
    width = state.shape[1]
    before_col = pltpu.roll(state, 1, 1)
    after_col = pltpu.roll(state, width - 1, 1)
    return left_w * before_col + mid_w * state + right_w * after_col


def split(value):
    high = value.astype(jnp.bfloat16)
    return high, (value - high.astype(jnp.float32)).astype(jnp.bfloat16)


def product(left, right):
    (left_high, left_low), (right_high, right_low) = left, right
    out = jnp.dot(left_high, right_high, preferred_element_type=jnp.float32)
    out = out + jnp.dot(left_high, right_low, preferred_element_type=jnp.float32)
    return out + jnp.dot(left_low, right_high, preferred_element_type=jnp.float32)


def weight_row(keep_ref, side, row, rows):
    return keep_ref[pl.ds(row + side * rows, 1), :]


def pushed(feat_ref, keep_ref, row, rows):
    return weight_row(keep_ref, 3, row, rows) * feat_ref[row].astype(jnp.float32)


def advanced(state, push, keep_ref, row, rows):
    return stencil(state, *[weight_row(keep_ref, side, row, rows) for side in range(3)]) + push


def summary_kernel(
    _, mix_hbm, decay_hbm, feat_hbm, gate_hbm, pack_ref, keep_ref, feat_ref, gate_ref,
    mix_ref, decay_ref, sem_ref, side_ref, diag_ref, dense_ref, pair_ref,
):
    copies = [
        pltpu.make_async_copy(source, target, sem_ref.at[k])
        for k, (source, target) in enumerate(
            ((mix_hbm, mix_ref), (decay_hbm, decay_ref), (feat_hbm, feat_ref), (gate_hbm, gate_ref))
        )
    ]
    for copy in copies:
        copy.start()
    copies[0].wait()
    copies[1].wait()
    rows, width = decay_ref.shape
    decay = decay_ref[...]
    retain = 1.0 - decay
    for side in range(3):
        value = retain * mix_ref[side]
        keep_ref[side * rows : (side + 1) * rows] = value
        for part in range(width // LANES):
            side_ref[side, part] = value[:, part * LANES : (part + 1) * LANES]
    keep_ref[3 * rows : 4 * rows] = jnp.sqrt(decay)

    blocks = rows // BLOCK

    def weights(j):
        row = pl.ds(j, blocks, stride=BLOCK)
        return [
            jnp.concatenate([side_ref[side, part, row, :] for part in range(width // LANES)], axis=1)
            for side in range(3)
        ]

    left_w, mid_w, right_w = weights(0)
    diagonals = {-1: left_w, 0: mid_w, 1: right_w}
    for j in range(1, BLOCK):
        left_w, mid_w, right_w = weights(j)
        news = {}
        for d, values in diagonals.items():
            terms = (
                (d - 1, left_w * pltpu.roll(values, 1, 1)),
                (d, mid_w * values),
                (d + 1, right_w * pltpu.roll(values, width - 1, 1)),
            )
            for to, term in terms:
                news[to] = news[to] + term if to in news else term
        diagonals = news
    for d, values in diagonals.items():
        diag_ref[d + BLOCK] = values

    lead = lax.broadcasted_iota(jnp.int32, (SUBLANES, LANES), 1) - lax.broadcasted_iota(
        jnp.int32, (SUBLANES, LANES), 0
    )
    for b in range(2):
        dense_ref[b] = jnp.zeros((width, width), jnp.float32)

    def pair(q):
        for left in range(0, width, LANES):
            lanes = slice(left, left + LANES)
            for top in range(max(0, left - SUBLANES), min(width, left + LANES + SUBLANES), SUBLANES):
                tiles = [jnp.zeros((SUBLANES, LANES), jnp.float32)] * 2
                for d in range(-BLOCK, BLOCK + 1):
                    offset = top - d - left
                    if -SUBLANES < offset < LANES:
                        here = lead == offset
                        for b in range(2):
                            row = diag_ref[d + BLOCK, pl.ds(2 * q + b, 1), :][:, lanes]
                            tiles[b] = jnp.where(here, jnp.broadcast_to(row, here.shape), tiles[b])
                for b in range(2):
                    dense_ref[b, top : top + SUBLANES, lanes] = tiles[b]
        high, low = split(product(split(dense_ref[0]), split(dense_ref[1])))
        pair_ref[q, 0] = high
        pair_ref[q, 1] = low

    copies[2].wait()
    channels = feat_ref.shape[1]
    half_rows = rows // 2
    pairs = blocks // 2
    each = half_rows // pairs

    def turn(q, states):
        for j in range(each):
            both = [q * each + j + half * half_rows for half in range(2)]
            states = tuple(
                advanced(state, pushed(feat_ref, keep_ref, row, rows), keep_ref, row, rows)
                for state, row in zip(states, both)
            )
        pair(q)
        return states

    zero = jnp.zeros((channels, width), jnp.float32)
    first, second = lax.fori_loop(0, pairs, turn, (zero, zero))
    early = product((pair_ref[0, 0], pair_ref[0, 1]), (pair_ref[1, 0], pair_ref[1, 1]))
    late = split(product((pair_ref[2, 0], pair_ref[2, 1]), (pair_ref[3, 0], pair_ref[3, 1])))
    keep_ref[4 * rows : 4 * rows + width] = early
    keep_ref[4 * rows + width : 4 * rows + width + channels] = first
    pack_ref[0:width] = product(split(early), late).astype(pack_ref.dtype)
    high, low = split(second + product(split(first), late))
    pack_ref[width : width + channels] = high
    pack_ref[width + channels : width + 2 * channels] = low
    copies[3].wait()


def summary(place, features, gate_input, mixing, decay_rate):
    rows, channels, width = features.shape
    vmem = pl.BlockSpec(memory_space=pltpu.VMEM)
    return pl.pallas_call(
        summary_kernel,
        in_specs=[pl.BlockSpec(memory_space=pltpu.SMEM)] + [pl.BlockSpec(memory_space=pltpu.HBM)] * 4,
        out_specs=[vmem] * 4,
        out_shape=(
            pltpu.VMEM((width + 2 * channels, width), jnp.bfloat16),
            pltpu.VMEM((4 * rows + width + channels, width), jnp.float32),
            pltpu.VMEM(features.shape, features.dtype),
            pltpu.VMEM(gate_input.shape, gate_input.dtype),
        ),
        scratch_shapes=[
            pltpu.VMEM(mixing.shape, jnp.float32),
            pltpu.VMEM(decay_rate.shape, jnp.float32),
            pltpu.SemaphoreType.DMA((4,)),
            pltpu.VMEM((3, width // LANES, rows, LANES), jnp.float32),
            pltpu.VMEM((2 * BLOCK + 1, rows // BLOCK, width), jnp.float32),
            pltpu.VMEM((2, width, width), jnp.float32),
            pltpu.VMEM((rows // BLOCK // 2, 2, width, width), jnp.bfloat16),
        ],
        cost_estimate=pl.CostEstimate(
            flops=14 * rows * channels * width, bytes_accessed=26 * MIB, transcendentals=0
        ),
        compiler_params=pltpu.CompilerParams(vmem_limit_bytes=16 * MIB),
        name="summary",
    )(place, *[pltpu.with_memory_space_constraint(a, pltpu.HBM) for a in (mixing, decay_rate, features, gate_input)])


def applied(state, operator):
    both = jnp.dot(jnp.concatenate(split(state)), operator, preferred_element_type=jnp.float32)
    return both[: state.shape[0]] + both[state.shape[0] :]


def unpacked(ref, width, channels):
    high = ref[width : width + channels].astype(jnp.float32)
    return high + ref[width + channels : width + 2 * channels].astype(jnp.float32)


def by_core(place_ref, mine_ref, theirs_ref, write):
    @pl.when(place_ref[0] == 0)
    def _():
        write(mine_ref, theirs_ref)

    @pl.when(place_ref[0] != 0)
    def _():
        write(theirs_ref, mine_ref)


def chip_end_kernel(place_ref, mine_ref, theirs_ref, end_ref, sent_ref):
    channels, width = end_ref.shape

    def write(earlier_ref, later_ref):
        end = applied(unpacked(earlier_ref, width, channels), later_ref[0:width])
        end = end + unpacked(later_ref, width, channels)
        end_ref[...] = end
        sent_ref[...] = end.astype(sent_ref.dtype)

    by_core(place_ref, mine_ref, theirs_ref, write)


def composite_kernel(place_ref, mine_ref, theirs_ref, end_ref, on_ref):
    channels, width = end_ref.shape
    high, low = split(end_ref[...])
    on_ref[width : width + channels] = high
    on_ref[width + channels : width + 2 * channels] = low

    def write(earlier_ref, later_ref):
        both = jnp.dot(earlier_ref[0:width], later_ref[0:width], preferred_element_type=jnp.float32)
        on_ref[0:width] = both.astype(on_ref.dtype)

    by_core(place_ref, mine_ref, theirs_ref, write)


def small_call(kernel, out_shape, place, *arrays):
    vmem = pl.BlockSpec(memory_space=pltpu.VMEM)
    return pl.pallas_call(
        kernel,
        in_specs=[pl.BlockSpec(memory_space=pltpu.SMEM)] + [vmem] * len(arrays),
        out_specs=jax.tree.map(lambda _: vmem, out_shape),
        out_shape=out_shape,
        cost_estimate=pl.CostEstimate(flops=2 * arrays[0].size * 256, bytes_accessed=2 * MIB, transcendentals=0),
        compiler_params=pltpu.CompilerParams(vmem_limit_bytes=4 * MIB),
    )(place, *arrays)


def chip_end_of(place, mine, theirs):
    width = mine.shape[1]
    shape = ((mine.shape[0] - width) // 2, width)
    out_shape = (jax.ShapeDtypeStruct(shape, jnp.float32), jax.ShapeDtypeStruct(shape, mine.dtype))
    return small_call(chip_end_kernel, out_shape, place, mine, theirs)


def composite_of(place, mine, theirs, end):
    out_shape = jax.ShapeDtypeStruct(mine.shape, mine.dtype)
    return small_call(composite_kernel, out_shape, place, mine, theirs, end)


def prepare_kernel(keep_ref, feat_ref, gate_ref, push_ref, silu_ref):
    rows = feat_ref.shape[0]

    def step(row, _):
        push_ref[row] = pushed(feat_ref, keep_ref, row, rows)
        gate = gate_ref[row].astype(jnp.float32)
        silu_ref[row] = gate / (1.0 + jnp.exp(-gate))
        return 0

    lax.fori_loop(0, rows, step, 0, unroll=UNROLL)


def prepare(keep, features, gate_input):
    vmem = pl.BlockSpec(memory_space=pltpu.VMEM)
    return pl.pallas_call(
        prepare_kernel,
        in_specs=[vmem] * 3,
        out_specs=[vmem] * 2,
        out_shape=[pltpu.VMEM(features.shape, jnp.float32)] * 2,
        cost_estimate=pl.CostEstimate(
            flops=8 * features.size, bytes_accessed=6 * MIB, transcendentals=2 * features.size
        ),
        compiler_params=pltpu.CompilerParams(vmem_limit_bytes=8 * MIB),
        name="prepare",
    )(keep, features, gate_input)


def carry_kernel(before_ref, on_ref, end_ref, out_ref):
    carried = jnp.dot(before_ref[...], on_ref[0 : out_ref.shape[1]], preferred_element_type=jnp.float32)
    out_ref[...] = (carried + end_ref[...]).astype(out_ref.dtype)


def carry(before, on, chip_end):
    vmem = pl.BlockSpec(memory_space=pltpu.VMEM)
    return pl.pallas_call(
        carry_kernel,
        in_specs=[vmem] * 3,
        out_specs=vmem,
        out_shape=jax.ShapeDtypeStruct(chip_end.shape, before.dtype),
        cost_estimate=pl.CostEstimate(flops=2 * on.size, bytes_accessed=2 * MIB, transcendentals=0),
        compiler_params=pltpu.CompilerParams(vmem_limit_bytes=4 * MIB),
        name="carry",
    )(before, on, chip_end)


def gated_kernel(
    place_ref, before_ref, near_ref, far_ref, beyond_ref, theirs_ref, keep_ref, push_ref, silu_ref, out_ref
):
    rows, channels, width = push_ref.shape
    farther = jnp.dot(far_ref[...], beyond_ref[0:width], preferred_element_type=jnp.float32)
    farther = farther + unpacked(beyond_ref, width, channels)
    incoming = before_ref[...].astype(jnp.float32) + near_ref[...].astype(jnp.float32) + farther
    later = applied(incoming, theirs_ref[0:width]) + unpacked(theirs_ref, width, channels)
    incoming = jnp.where(place_ref[0] == 0, incoming, later)
    early = keep_ref[4 * rows : 4 * rows + width]
    second = keep_ref[4 * rows + width : 4 * rows + width + channels] + product(split(incoming), split(early))

    def step(i, states):
        news = []
        for half in range(2):
            row = i + half * (rows // 2)
            news.append(advanced(states[half], push_ref[row], keep_ref, row, rows))
            out_ref[row] = (news[half] * silu_ref[row]).astype(out_ref.dtype)
        return tuple(news)

    lax.fori_loop(0, rows // 2, step, (incoming, second), unroll=UNROLL)


def gated(place, starts, push, silu):
    rows, channels, width = push.shape
    vmem = pl.BlockSpec(memory_space=pltpu.VMEM)
    return pl.pallas_call(
        gated_kernel,
        in_specs=[pl.BlockSpec(memory_space=pltpu.SMEM)] + [vmem] * (len(starts) + 2),
        out_specs=vmem,
        out_shape=jax.ShapeDtypeStruct(push.shape, jnp.bfloat16),
        cost_estimate=pl.CostEstimate(
            flops=48 * rows * channels * width,
            bytes_accessed=24 * rows * channels * width,
            transcendentals=8 * rows * channels * width,
        ),
        compiler_params=pltpu.CompilerParams(vmem_limit_bytes=8 * MIB),
        name="gated",
    )(place, *starts, push, silu)


def project_kernel(weight_ref, gated_ref, out_ref, done_ref, sem_ref):
    peers, rows, channels, width = gated_ref.shape
    outs = weight_ref.shape[0]
    tile = outs // TILES
    copies = []
    for row in range(rows):
        here = gated_ref[:, row].reshape(peers * channels, width)
        for t in range(TILES):
            part = pl.ds(t * tile, tile)
            done_ref[row, part, :] = jnp.dot(
                weight_ref[part, :], here, preferred_element_type=jnp.float32
            ).astype(done_ref.dtype)
            copy = pltpu.make_async_copy(done_ref.at[row, part], out_ref.at[row, part], sem_ref.at[row, t])
            copy.start()
            copies.append(copy)
    for copy in copies:
        copy.wait()


def project(out_weight, gathered):
    _, rows, _, width = gathered.shape
    outs = out_weight.shape[0]
    return pl.pallas_call(
        project_kernel,
        in_specs=[pl.BlockSpec(memory_space=pltpu.VMEM)] * 2,
        out_specs=pl.BlockSpec(memory_space=pl.ANY),
        out_shape=jax.ShapeDtypeStruct((rows, outs, width), jnp.bfloat16),
        scratch_shapes=[
            pltpu.VMEM((rows, outs, width), jnp.bfloat16),
            pltpu.SemaphoreType.DMA((rows, TILES)),
        ],
        compiler_params=pltpu.CompilerParams(vmem_limit_bytes=8 * MIB),
        cost_estimate=pl.CostEstimate(
            flops=2 * rows * outs * outs * width, bytes_accessed=4 * outs * outs, transcendentals=0
        ),
        name="project",
    )(out_weight, gathered)


def shards(slabs, peers, features, mixing, decay_rate, gate_input, out_weight):
    rows, channels, width = features.shape
    place = lax.axis_index("rows").astype(jnp.int32)
    place = jnp.stack([place % 2, place // 2])

    def chip_to(value, *pairs):
        return lax.ppermute(value, "rows", [(2 * a + c, 2 * b + c) for a, b in pairs for c in range(2)])

    mine, keep, features, gate_input = summary(place, features, gate_input, mixing, decay_rate)
    theirs = lax.ppermute(mine, "rows", [(i, i ^ 1) for i in range(slabs)])
    chip_end, sent = chip_end_of(place, mine, theirs)
    before = chip_to(sent, (0, 1))
    on = composite_of(place, mine, theirs, chip_end)
    beyond = chip_to(on, (2, 3))
    push, silu = prepare(keep, features, gate_input)
    carried = carry(before, on, chip_end)
    far = chip_to(carried, (1, 3))
    near = chip_to(carried, (1, 2))

    starts = (before, near, far, beyond, theirs, keep)
    mixed = gated(place, starts, push, silu)
    mixed = mixed.reshape(peers, rows // peers, channels, width)
    return project(out_weight, lax.all_to_all(mixed, "chan", split_axis=0, concat_axis=0, tiled=True))


def solution(mesh):
    in_specs = (
        P("rows", "chan", None),
        P(None, "rows", None),
        P("rows", None),
        P("rows", "chan", None),
        P(),
    )
    out_specs = P(("rows", "chan"), None, None)

    def whole(features, mixing, decay_rate, gate_input, out_weight):
        return shards(
            mesh.shape["rows"], mesh.shape["chan"], features, mixing, decay_rate, gate_input, out_weight
        )

    return jax.shard_map(whole, mesh=mesh, in_specs=in_specs, out_specs=out_specs, check_vma=False)
```

```python
import jax
import jax.numpy as jnp
from jax import lax
from jax.experimental import pallas as pl
from jax.experimental.pallas import tpu as pltpu
from jax.sharding import PartitionSpec as P

UNROLL = 32
BLOCK = 8
SUBLANES = 8
LANES = 128
TILES = 4
MIB = 1024 * 1024


def stencil(state, left_w, mid_w, right_w):
    width = state.shape[1]
    before_col = pltpu.roll(state, 1, 1)
    after_col = pltpu.roll(state, width - 1, 1)
    return left_w * before_col + mid_w * state + right_w * after_col


def split(value):
    high = value.astype(jnp.bfloat16)
    return high, (value - high.astype(jnp.float32)).astype(jnp.bfloat16)


def product(left, right):
    (left_high, left_low), (right_high, right_low) = left, right
    out = jnp.dot(left_high, right_high, preferred_element_type=jnp.float32)
    out = out + jnp.dot(left_high, right_low, preferred_element_type=jnp.float32)
    return out + jnp.dot(left_low, right_high, preferred_element_type=jnp.float32)


def advance(i, states, feat_ref, keep_ref, rows, take=None):
    news = []
    for half in range(2):
        row = i + half * rows
        left_w, mid_w, right_w, in_w = [keep_ref[pl.ds(row + k * 2 * rows, 1), :] for k in range(4)]
        push = in_w * feat_ref[row].astype(jnp.float32)
        news.append(stencil(states[half], left_w, mid_w, right_w) + push)
        if take is not None:
            take(row, news[half])
    return tuple(news)


def summary_kernel(
    _, mix_hbm, decay_hbm, feat_hbm, gate_hbm, pack_ref, keep_ref, feat_ref, gate_ref,
    mix_ref, decay_ref, sem_ref, side_ref, diag_ref, dense_ref, pair_ref,
):
    copies = [
        pltpu.make_async_copy(source, target, sem_ref.at[k])
        for k, (source, target) in enumerate(
            ((mix_hbm, mix_ref), (decay_hbm, decay_ref), (feat_hbm, feat_ref), (gate_hbm, gate_ref))
        )
    ]
    for copy in copies:
        copy.start()
    copies[0].wait()
    copies[1].wait()
    rows, width = decay_ref.shape
    decay = decay_ref[...]
    retain = 1.0 - decay
    for side in range(3):
        value = retain * mix_ref[side]
        keep_ref[side * rows : (side + 1) * rows] = value
        for part in range(width // LANES):
            side_ref[side, part] = value[:, part * LANES : (part + 1) * LANES]
    keep_ref[3 * rows : 4 * rows] = jnp.sqrt(decay)

    blocks = rows // BLOCK

    def weights(j):
        row = pl.ds(j, blocks, stride=BLOCK)
        return [
            jnp.concatenate([side_ref[side, part, row, :] for part in range(width // LANES)], axis=1)
            for side in range(3)
        ]

    left_w, mid_w, right_w = weights(0)
    diagonals = {-1: left_w, 0: mid_w, 1: right_w}
    for j in range(1, BLOCK):
        left_w, mid_w, right_w = weights(j)
        news = {}
        for d, values in diagonals.items():
            terms = (
                (d - 1, left_w * pltpu.roll(values, 1, 1)),
                (d, mid_w * values),
                (d + 1, right_w * pltpu.roll(values, width - 1, 1)),
            )
            for to, term in terms:
                news[to] = news[to] + term if to in news else term
        diagonals = news
    for d, values in diagonals.items():
        diag_ref[d + BLOCK] = values

    lead = lax.broadcasted_iota(jnp.int32, (SUBLANES, LANES), 1) - lax.broadcasted_iota(
        jnp.int32, (SUBLANES, LANES), 0
    )
    for b in range(2):
        dense_ref[b] = jnp.zeros((width, width), jnp.float32)

    def pair(q):
        for left in range(0, width, LANES):
            lanes = slice(left, left + LANES)
            for top in range(max(0, left - SUBLANES), min(width, left + LANES + SUBLANES), SUBLANES):
                tiles = [jnp.zeros((SUBLANES, LANES), jnp.float32)] * 2
                for d in range(-BLOCK, BLOCK + 1):
                    offset = top - d - left
                    if -SUBLANES < offset < LANES:
                        here = lead == offset
                        for b in range(2):
                            row = diag_ref[d + BLOCK, pl.ds(2 * q + b, 1), :][:, lanes]
                            tiles[b] = jnp.where(here, jnp.broadcast_to(row, here.shape), tiles[b])
                for b in range(2):
                    dense_ref[b, top : top + SUBLANES, lanes] = tiles[b]
        high, low = split(product(split(dense_ref[0]), split(dense_ref[1])))
        pair_ref[q, 0] = high
        pair_ref[q, 1] = low

    copies[2].wait()
    channels = feat_ref.shape[1]
    half_rows = rows // 2
    pairs = blocks // 2
    each = half_rows // pairs

    def turn(q, states):
        for j in range(each):
            states = advance(q * each + j, states, feat_ref, keep_ref, half_rows)
        pair(q)
        return states

    zero = jnp.zeros((channels, width), jnp.float32)
    first, second = lax.fori_loop(0, pairs, turn, (zero, zero))
    early = product((pair_ref[0, 0], pair_ref[0, 1]), (pair_ref[1, 0], pair_ref[1, 1]))
    late = split(product((pair_ref[2, 0], pair_ref[2, 1]), (pair_ref[3, 0], pair_ref[3, 1])))
    keep_ref[4 * rows : 4 * rows + width] = early
    keep_ref[4 * rows + width : 4 * rows + width + channels] = first
    pack_ref[0:width] = product(split(early), late).astype(pack_ref.dtype)
    high, low = split(second + product(split(first), late))
    pack_ref[width : width + channels] = high
    pack_ref[width + channels : width + 2 * channels] = low
    copies[3].wait()


def summary(place, features, gate_input, mixing, decay_rate):
    rows, channels, width = features.shape
    vmem = pl.BlockSpec(memory_space=pltpu.VMEM)
    return pl.pallas_call(
        summary_kernel,
        in_specs=[pl.BlockSpec(memory_space=pltpu.SMEM)] + [pl.BlockSpec(memory_space=pltpu.HBM)] * 4,
        out_specs=[vmem] * 4,
        out_shape=(
            pltpu.VMEM((width + 2 * channels, width), jnp.bfloat16),
            pltpu.VMEM((4 * rows + width + channels, width), jnp.float32),
            pltpu.VMEM(features.shape, features.dtype),
            pltpu.VMEM(gate_input.shape, gate_input.dtype),
        ),
        scratch_shapes=[
            pltpu.VMEM(mixing.shape, jnp.float32),
            pltpu.VMEM(decay_rate.shape, jnp.float32),
            pltpu.SemaphoreType.DMA((4,)),
            pltpu.VMEM((3, width // LANES, rows, LANES), jnp.float32),
            pltpu.VMEM((2 * BLOCK + 1, rows // BLOCK, width), jnp.float32),
            pltpu.VMEM((2, width, width), jnp.float32),
            pltpu.VMEM((rows // BLOCK // 2, 2, width, width), jnp.bfloat16),
        ],
        cost_estimate=pl.CostEstimate(
            flops=14 * rows * channels * width, bytes_accessed=26 * MIB, transcendentals=0
        ),
        compiler_params=pltpu.CompilerParams(vmem_limit_bytes=16 * MIB),
        name="summary",
    )(place, *[pltpu.with_memory_space_constraint(a, pltpu.HBM) for a in (mixing, decay_rate, features, gate_input)])


def applied(state, operator):
    both = jnp.dot(jnp.concatenate(split(state)), operator, preferred_element_type=jnp.float32)
    return both[: state.shape[0]] + both[state.shape[0] :]


def unpacked(ref, width, channels):
    high = ref[width : width + channels].astype(jnp.float32)
    return high + ref[width + channels : width + 2 * channels].astype(jnp.float32)


def chip_kernel(place_ref, mine_ref, theirs_ref, on_ref, end_ref, sent_ref):
    channels, width = end_ref.shape

    def write(earlier_ref, later_ref):
        later_op = later_ref[0:width]
        end = applied(unpacked(earlier_ref, width, channels), later_op) + unpacked(later_ref, width, channels)
        end_ref[...] = end
        high, low = split(end)
        sent_ref[...] = high
        on_ref[width : width + channels] = high
        on_ref[width + channels : width + 2 * channels] = low
        both = jnp.dot(earlier_ref[0:width], later_op, preferred_element_type=jnp.float32)
        on_ref[0:width] = both.astype(on_ref.dtype)

    @pl.when(place_ref[0] == 0)
    def _():
        write(mine_ref, theirs_ref)

    @pl.when(place_ref[0] != 0)
    def _():
        write(theirs_ref, mine_ref)


def chip_of(place, mine, theirs):
    width = mine.shape[1]
    channels = (mine.shape[0] - width) // 2
    vmem = pl.BlockSpec(memory_space=pltpu.VMEM)
    return pl.pallas_call(
        chip_kernel,
        in_specs=[pl.BlockSpec(memory_space=pltpu.SMEM), vmem, vmem],
        out_specs=(vmem, vmem, vmem),
        out_shape=(
            jax.ShapeDtypeStruct(mine.shape, mine.dtype),
            jax.ShapeDtypeStruct((channels, width), jnp.float32),
            jax.ShapeDtypeStruct((channels, width), mine.dtype),
        ),
        cost_estimate=pl.CostEstimate(flops=2 * width**3, bytes_accessed=4 * MIB, transcendentals=0),
        compiler_params=pltpu.CompilerParams(vmem_limit_bytes=4 * MIB),
        name="chip",
    )(place, mine, theirs)


def carry_kernel(before_ref, on_ref, end_ref, out_ref):
    carried = jnp.dot(before_ref[...], on_ref[0 : out_ref.shape[1]], preferred_element_type=jnp.float32)
    out_ref[...] = (carried + end_ref[...]).astype(out_ref.dtype)


def carry(before, on, chip_end):
    vmem = pl.BlockSpec(memory_space=pltpu.VMEM)
    return pl.pallas_call(
        carry_kernel,
        in_specs=[vmem] * 3,
        out_specs=vmem,
        out_shape=jax.ShapeDtypeStruct(chip_end.shape, before.dtype),
        cost_estimate=pl.CostEstimate(flops=2 * on.size, bytes_accessed=2 * MIB, transcendentals=0),
        compiler_params=pltpu.CompilerParams(vmem_limit_bytes=4 * MIB),
        name="carry",
    )(before, on, chip_end)


def gated_kernel(
    place_ref, before_ref, near_ref, far_ref, beyond_ref, theirs_ref, keep_ref, feat_ref, gate_ref, out_ref
):
    rows, channels, width = feat_ref.shape
    farther = jnp.dot(far_ref[...], beyond_ref[0:width], preferred_element_type=jnp.float32)
    farther = farther + unpacked(beyond_ref, width, channels)
    incoming = before_ref[...].astype(jnp.float32) + near_ref[...].astype(jnp.float32) + farther
    later = applied(incoming, theirs_ref[0:width]) + unpacked(theirs_ref, width, channels)
    incoming = jnp.where(place_ref[0] == 0, incoming, later)
    early = keep_ref[4 * rows : 4 * rows + width]
    second = keep_ref[4 * rows + width : 4 * rows + width + channels] + product(split(incoming), split(early))

    def take(row, state):
        gate = gate_ref[row].astype(jnp.float32)
        out_ref[row] = (state * (gate / (1.0 + jnp.exp(-gate)))).astype(out_ref.dtype)

    def step(i, states):
        return advance(i, states, feat_ref, keep_ref, rows // 2, take)

    lax.fori_loop(0, rows // 2, step, (incoming, second), unroll=UNROLL)


def gated(place, starts, features, gate_input):
    rows, channels, width = features.shape
    vmem = pl.BlockSpec(memory_space=pltpu.VMEM)
    return pl.pallas_call(
        gated_kernel,
        in_specs=[pl.BlockSpec(memory_space=pltpu.SMEM)] + [vmem] * (len(starts) + 2),
        out_specs=vmem,
        out_shape=jax.ShapeDtypeStruct(features.shape, jnp.bfloat16),
        cost_estimate=pl.CostEstimate(
            flops=48 * rows * channels * width,
            bytes_accessed=24 * rows * channels * width,
            transcendentals=8 * rows * channels * width,
        ),
        compiler_params=pltpu.CompilerParams(vmem_limit_bytes=8 * MIB),
        name="gated",
    )(place, *starts, features, gate_input)


def project_kernel(weight_ref, gated_ref, out_ref, done_ref, sem_ref):
    peers, rows, channels, width = gated_ref.shape
    outs = weight_ref.shape[0]
    tile = outs // TILES
    copies = []
    for row in range(rows):
        here = gated_ref[:, row].reshape(peers * channels, width)
        for t in range(TILES):
            part = pl.ds(t * tile, tile)
            done_ref[row, part, :] = jnp.dot(
                weight_ref[part, :], here, preferred_element_type=jnp.float32
            ).astype(done_ref.dtype)
            copy = pltpu.make_async_copy(done_ref.at[row, part], out_ref.at[row, part], sem_ref.at[row, t])
            copy.start()
            copies.append(copy)
    for copy in copies:
        copy.wait()


def project(out_weight, gathered):
    _, rows, _, width = gathered.shape
    outs = out_weight.shape[0]
    return pl.pallas_call(
        project_kernel,
        in_specs=[pl.BlockSpec(memory_space=pltpu.VMEM)] * 2,
        out_specs=pl.BlockSpec(memory_space=pl.ANY),
        out_shape=jax.ShapeDtypeStruct((rows, outs, width), jnp.bfloat16),
        scratch_shapes=[
            pltpu.VMEM((rows, outs, width), jnp.bfloat16),
            pltpu.SemaphoreType.DMA((rows, TILES)),
        ],
        compiler_params=pltpu.CompilerParams(vmem_limit_bytes=8 * MIB),
        cost_estimate=pl.CostEstimate(
            flops=2 * rows * outs * outs * width, bytes_accessed=4 * outs * outs, transcendentals=0
        ),
        name="project",
    )(out_weight, gathered)


def shards(slabs, peers, features, mixing, decay_rate, gate_input, out_weight):
    rows, channels, width = features.shape
    place = lax.axis_index("rows").astype(jnp.int32)
    place = jnp.stack([place % 2, place // 2])

    def chip_to(value, *pairs):
        return lax.ppermute(value, "rows", [(2 * a + c, 2 * b + c) for a, b in pairs for c in range(2)])

    mine, keep, features, gate_input = summary(place, features, gate_input, mixing, decay_rate)
    theirs = lax.ppermute(mine, "rows", [(i, i ^ 1) for i in range(slabs)])
    on, chip_end, sent = chip_of(place, mine, theirs)
    before = chip_to(sent, (0, 1))
    beyond = chip_to(on, (2, 3))
    carried = carry(before, on, chip_end)
    far = chip_to(carried, (1, 3))
    near = chip_to(carried, (1, 2))

    starts = (before, near, far, beyond, theirs, keep)
    mixed = gated(place, starts, features, gate_input)
    mixed = mixed.reshape(peers, rows // peers, channels, width)
    return project(out_weight, lax.all_to_all(mixed, "chan", split_axis=0, concat_axis=0, tiled=True))


def solution(mesh):
    in_specs = (
        P("rows", "chan", None),
        P(None, "rows", None),
        P("rows", None),
        P("rows", "chan", None),
        P(),
    )
    out_specs = P(("rows", "chan"), None, None)

    def whole(features, mixing, decay_rate, gate_input, out_weight):
        return shards(
            mesh.shape["rows"], mesh.shape["chan"], features, mixing, decay_rate, gate_input, out_weight
        )

    return jax.shard_map(whole, mesh=mesh, in_specs=in_specs, out_specs=out_specs, check_vma=False)
```
